256 devices in a mesh: dp: 4 (over z_lo, core), ang: 4 (over y), rows: 16 (over z_hi, x).
Axes of the slice: x: 4, y: 4, z: 8 (z_hi: 4, z_lo: 2; z = z_hi * 2 + z_lo), core: 2. Of those that a mesh axis runs over, the one named last changes fastest.
Arguments:
- light_field: bfloat16 [4, 1, 8, 64, 64, 512], P('dp', None, 'ang', 'rows'), may hold values from -6 to 6
- spatial_weight: bfloat16 [3, 3, 64, 64], replicated, may hold values from -0.25 to 0.25
- epi_weight: bfloat16 [3, 3, 64, 64], replicated, may hold values from -0.25 to 0.25
- upsample_weight: bfloat16 [16, 64], replicated, may hold values from -0.75 to 0.75
- image_grad: bfloat16 [4, 1, 8, 256, 2048], P('dp', None, 'ang', 'rows'), may hold values from -0.005859375 to 0.005859375
Outputs:
- upscaled: bfloat16 [4, 1, 8, 256, 2048], P('dp', None, 'ang', 'rows')
- spatial_grad: float32 [3, 3, 64, 64], replicated
- epi_grad: float32 [3, 3, 64, 64], replicated
- upsample_grad: float32 [16, 64], replicated
The draws below stay inside these ranges and needn't reach their ends.
All inputs are finite; a program needn't handle non-finite values.
Results may differ from the reference program's by a relative error of at most 0.0066.
Values may be sent and summed in bfloat16 or wider, within the bound.
No kernel may reach another device: no remote copies, remote signals or barrier semaphores. Data moves between devices by JAX's collectives and lax.ppermute only.
A program may use at most 64 MiB of HBM per device.

```python
import jax
import jax.numpy as jnp
from jax import lax

C = 64
SCALE = 4
SUB = 16
U = 1
V = 8
W = 512
BATCH = 4
H = 64
PIXELS = 1048576


def block_scale(rng, dims, cuts, low, top_value):
    factor_of, own = 1.0, jax.random.fold_in(rng, 6)
    for dim, shards_of in cuts:
        draws = jnp.exp(jax.random.uniform(jax.random.fold_in(own, dim), (shards_of,), jnp.float32, low / len(cuts), top_value / len(cuts)))
        factor_of = factor_of * jnp.repeat(draws, dims[dim] // shards_of).reshape([-1 if axis == dim else 1 for axis in range(len(dims))])
    return factor_of


def normal_values(key, shape, spread, reach, cuts=(), kind=jnp.bfloat16):
    level = block_scale(key, shape, cuts, -0.22, 0.18) if cuts else 1.0
    array = jax.random.normal(key, shape, jnp.float32) * spread * level
    return jnp.minimum(jnp.maximum(array, -reach), reach).astype(kind)


def setup_inputs(seed: int = 0) -> dict:
    seeds = jax.random.split(jax.random.key(seed), 6)
    return {
        "light_field": normal_values(seeds[0], (BATCH, U, V, H, C, W), 1.0, 6.0, ((0, 4), (2, 4), (3, 16))),
        "spatial_weight": normal_values(seeds[1], (3, 3, C, C), (9 * C) ** -0.5, 0.25),
        "epi_weight": normal_values(seeds[2], (3, 3, C, C), (9 * C) ** -0.5, 0.25),
        "upsample_weight": normal_values(seeds[3], (SUB, C), C ** -0.5, 0.75),
        "image_grad": normal_values(seeds[4], (BATCH, U, V, H * SCALE, W * SCALE), (1.0 / PIXELS ** 0.5), 0.005859375, ((0, 4), (2, 4), (3, 16))),
    }


def silu_slope(values):
    sigmoid_value = jax.nn.sigmoid(values)
    return sigmoid_value * (1.0 + values * (1.0 - sigmoid_value))

def spatial_conv(padded, weight):
    height = padded.shape[1] - 2
    breadth = padded.shape[3] - 2
    summed = jnp.zeros((padded.shape[0], height, weight.shape[2], breadth), jnp.float32)
    for tap_row in range(3):
        for tap_col in range(3):
            summed = summed + jnp.einsum('oc,vhcw->vhow', weight[tap_row, tap_col], padded[:, tap_row:tap_row + height, :, tap_col:tap_col + breadth])
    return summed

def epi_conv(padded, weight):
    views_all = padded.shape[0] - 2
    breadth = padded.shape[3] - 2
    summed = jnp.zeros((views_all, padded.shape[1], weight.shape[2], breadth), jnp.float32)
    for tap_row in range(3):
        for tap_col in range(3):
            summed = summed + jnp.einsum('oc,vhcw->vhow', weight[tap_row, tap_col], padded[tap_row:tap_row + views_all, :, :, tap_col:tap_col + breadth])
    return summed

def epi_back(padded, weight):
    views_all = padded.shape[0] - 2
    breadth = padded.shape[3] - 2
    summed = jnp.zeros((views_all, padded.shape[1], weight.shape[3], breadth), jnp.float32)
    for tap_row in range(3):
        for tap_col in range(3):
            summed = summed + jnp.einsum('oc,vhow->vhcw', weight[tap_row, tap_col], padded[2 - tap_row:2 - tap_row + views_all, :, :, 2 - tap_col:2 - tap_col + breadth])
    return summed

def weight_grad(upstream, padded, along_dim):
    extent = upstream.shape[along_dim]
    breadth = upstream.shape[3]
    rows_out = []
    for tap_row in range(3):
        row_list = []
        for tap_col in range(3):
            window = lax.slice_in_dim(padded, tap_row, tap_row + extent, axis=along_dim)
            window = lax.slice_in_dim(window, tap_col, tap_col + breadth, axis=3)
            row_list.append(jnp.einsum('vhow,vhcw->oc', upstream, window))
        rows_out.append(jnp.stack(row_list))
    return jnp.stack(rows_out)

def reference(light_field, spatial_weight, epi_weight, upsample_weight, image_grad):
    spatial_w = spatial_weight.astype(jnp.float32)
    epi_w = epi_weight.astype(jnp.float32)
    up_w = upsample_weight.astype(jnp.float32)

    def one_field(carried, inputs):
        field, image = inputs
        spatial_in = jnp.pad(field.astype(jnp.float32), ((0, 0), (1, 1), (0, 0), (1, 1)))
        spatial_out = spatial_conv(spatial_in, spatial_w)
        first = (field.astype(jnp.float32) + jax.nn.silu(spatial_out)).astype(jnp.bfloat16)
        epi_in = jnp.pad(first.astype(jnp.float32), ((1, 1), (0, 0), (0, 0), (1, 1)))
        epi_out = epi_conv(epi_in, epi_w)
        second = (first.astype(jnp.float32) + jax.nn.silu(epi_out)).astype(jnp.bfloat16)
        lifted = jnp.einsum('sc,vhcw->vhsw', up_w, second.astype(jnp.float32)).astype(jnp.bfloat16)
        shuffled = lifted.reshape(V, H, SCALE, SCALE, W).transpose(0, 1, 2, 4, 3).reshape(V, H * SCALE, W * SCALE)
        cotangent = image.reshape(V, H, SCALE, W, SCALE).transpose(0, 1, 2, 4, 3).reshape(V, H, SUB, W).astype(jnp.float32)
        up_part = jnp.einsum('vhsw,vhcw->sc', cotangent, second.astype(jnp.float32))
        second_grad = jnp.einsum('sc,vhsw->vhcw', up_w, cotangent).astype(jnp.bfloat16)
        epi_slope = (second_grad.astype(jnp.float32) * silu_slope(epi_out)).astype(jnp.bfloat16)
        epi_part = weight_grad(epi_slope.astype(jnp.float32), epi_in, 0)
        slope_pad = jnp.pad(epi_slope.astype(jnp.float32), ((1, 1), (0, 0), (0, 0), (1, 1)))
        first_grad = (second_grad.astype(jnp.float32) + epi_back(slope_pad, epi_w)).astype(jnp.bfloat16)
        spatial_slope = (first_grad.astype(jnp.float32) * silu_slope(spatial_out)).astype(jnp.bfloat16)
        spatial_part = weight_grad(spatial_slope.astype(jnp.float32), spatial_in, 1)
        return ((carried[0] + spatial_part, carried[1] + epi_part, carried[2] + up_part), shuffled)
    fields = light_field.reshape(BATCH * U, V, H, C, W)
    images = image_grad.reshape(BATCH * U, V, H * SCALE, W * SCALE)
    initial = (jnp.zeros((3, 3, C, C), jnp.float32), jnp.zeros((3, 3, C, C), jnp.float32), jnp.zeros((SUB, C), jnp.float32))
    carried, upscaled = lax.scan(one_field, initial, (fields, images))
    return (upscaled.reshape(BATCH, U, V, H * SCALE, W * SCALE), carried[0], carried[1], carried[2])
```

```python
import jax
import jax.numpy as jnp
from jax import lax
from jax.sharding import PartitionSpec as P

SCALE = 4
SUB = 16


def with_halo(cells, sides, width):
    for axis, dim in sides:
        count = lax.axis_size(axis)
        ends = count - 1
        head = lax.slice_in_dim(cells, 0, width, axis=dim)
        tail = lax.slice_in_dim(cells, cells.shape[dim] - width, cells.shape[dim], axis=dim)
        cells = jnp.concatenate(
            [
                lax.ppermute(tail, axis, [(i, (i + 1) % count) for i in range(ends)]),
                cells,
                lax.ppermute(head, axis, [((i + 1) % count, i) for i in range(ends)]),
            ],
            axis=dim,
        )
    return cells


def silu_slope(values):
    sigmoid_value = jax.nn.sigmoid(values)
    return sigmoid_value * (1.0 + values * (1.0 - sigmoid_value))


def spatial_conv(padded, weight, height, breadth):
    summed = jnp.zeros(padded.shape[:3] + (height, weight.shape[2], breadth), jnp.float32)
    for tap_row in range(3):
        for tap_col in range(3):
            summed = summed + jnp.einsum(
                "oc,buvhcw->buvhow",
                weight[tap_row, tap_col],
                padded[:, :, :, tap_row : tap_row + height, :, tap_col : tap_col + breadth],
                preferred_element_type=jnp.float32,
            )
    return summed


def epi_conv(padded, weight, views_all, breadth):
    summed = jnp.zeros(
        padded.shape[:2] + (views_all, padded.shape[3], weight.shape[2], breadth), jnp.float32
    )
    for tap_row in range(3):
        for tap_col in range(3):
            summed = summed + jnp.einsum(
                "oc,buvhcw->buvhow",
                weight[tap_row, tap_col],
                padded[:, :, tap_row : tap_row + views_all, :, :, tap_col : tap_col + breadth],
                preferred_element_type=jnp.float32,
            )
    return summed


def epi_back(padded, weight, views_all, breadth):
    summed = jnp.zeros(
        padded.shape[:2] + (views_all, padded.shape[3], weight.shape[3], breadth), jnp.float32
    )
    for tap_row in range(3):
        for tap_col in range(3):
            summed = summed + jnp.einsum(
                "oc,buvhow->buvhcw",
                weight[tap_row, tap_col],
                padded[
                    :,
                    :,
                    2 - tap_row : 2 - tap_row + views_all,
                    :,
                    :,
                    2 - tap_col : 2 - tap_col + breadth,
                ],
                preferred_element_type=jnp.float32,
            )
    return summed


def weight_grad(upstream, padded, along_dim, extent, breadth):
    rows_out = []
    for tap_row in range(3):
        row_list = []
        for tap_col in range(3):
            window = lax.slice_in_dim(padded, tap_row, tap_row + extent, axis=along_dim)
            window = lax.slice_in_dim(window, tap_col, tap_col + breadth, axis=5)
            row_list.append(
                jnp.einsum(
                    "buvhow,buvhcw->oc", upstream, window, preferred_element_type=jnp.float32
                )
            )
        rows_out.append(jnp.stack(row_list))
    return jnp.stack(rows_out)


def project_up(weight, features):
    return jnp.einsum(
        "sc,buvhcw->buvhsw", weight, features, preferred_element_type=jnp.float32
    ).astype(jnp.bfloat16)


def shift_pairs(kind, step):
    if kind == "x":
        return "rows", [(g * 4 + i, g * 4 + (i + step) % 4) for g in range(4) for i in range(4)]
    if kind == "z":
        return "rows", [(4 * i + g, 4 * ((i + step) % 4) + g) for g in range(4) for i in range(4)]
    return kind, [(i, (i + step) % 4) for i in range(4)]


def place_in(kind):
    if kind == "x":
        return lax.axis_index("rows") % 4
    if kind == "z":
        return lax.axis_index("rows") // 4
    return lax.axis_index(kind)


def shifted(value, kind, step):
    axis, pairs = shift_pairs(kind, step)
    return lax.ppermute(value, axis, pairs)


def gather_sum(value, kind):
    one, two, three = (shifted(value, kind, step) for step in (1, 2, 3))
    return (value + two) + (one + three)


def scatter_sum(value, kind):
    place = place_in(kind)
    mine = lax.dynamic_index_in_dim(value, place, 0, keepdims=False)
    one, two, three = (
        shifted(lax.dynamic_index_in_dim(value, (place + step) % 4, 0, keepdims=False), kind, step)
        for step in (1, 2, 3)
    )
    return (mine + two) + (one + three)


def gather_parts(value, kind):
    place = place_in(kind)
    around = jnp.stack([value] + [shifted(value, kind, step) for step in (1, 2, 3)])
    return jnp.concatenate(
        [lax.dynamic_index_in_dim(around, (place - part) % 4, 0) for part in range(4)], axis=0
    )


def sum_everywhere(parts):
    flat = jnp.concatenate([part.reshape(-1, 128) for part in parts], axis=0)
    rows = flat.shape[0]
    share = -(-rows // 32) * 8
    flat = jnp.pad(flat, ((0, 4 * share - rows), (0, 0))).reshape(4, share, 128)
    mine = scatter_sum(flat, "dp")
    for kind in ("x", "z", "ang"):
        mine = gather_sum(mine, kind)
    flat = gather_parts(mine, "dp").reshape(4 * share, 128)
    results, start = [], 0
    for part in parts:
        count = part.size // 128
        results.append(flat[start : start + count].reshape(part.shape))
        start += count
    return results


def on_device(light_field, spatial_weight, epi_weight, upsample_weight, image_grad):
    batch_here, angular_rows, views_here, rows_here, channels, breadth = light_field.shape
    rimmed = with_halo(light_field, (("rows", 3),), 1)
    spatial_in = jnp.pad(rimmed, ((0, 0), (0, 0), (0, 0), (0, 0), (0, 0), (1, 1)))
    spatial_out = spatial_conv(spatial_in, spatial_weight, rows_here, breadth)
    first = (light_field.astype(jnp.float32) + jax.nn.silu(spatial_out)).astype(jnp.bfloat16)
    cotangent = image_grad.reshape(
        batch_here, angular_rows, views_here, rows_here, SCALE, breadth, SCALE
    )
    cotangent = cotangent.transpose(0, 1, 2, 3, 4, 6, 5).reshape(
        batch_here, angular_rows, views_here, rows_here, SUB, breadth
    )
    epi_block = lax.all_to_all(first, "ang", split_axis=3, concat_axis=2, tiled=True)
    views_block = epi_block.shape[2]
    padded_block = jnp.pad(epi_block, ((0, 0), (0, 0), (1, 1), (0, 0), (0, 0), (1, 1)))
    block_out = epi_conv(padded_block, epi_weight, views_block, breadth)
    block_second = (epi_block.astype(jnp.float32) + jax.nn.silu(block_out)).astype(jnp.bfloat16)
    views_all = block_second.shape[2]
    second_views = lax.all_to_all(block_second, "ang", split_axis=2, concat_axis=3, tiled=True)
    lifted_views = project_up(upsample_weight, second_views)
    up_grad = jnp.einsum(
        "buvhsw,buvhcw->sc", cotangent, second_views, preferred_element_type=jnp.float32
    )
    view_grad = jnp.einsum(
        "sc,buvhsw->buvhcw", upsample_weight, cotangent, preferred_element_type=jnp.float32
    ).astype(jnp.bfloat16)
    second_grad = lax.all_to_all(view_grad, "ang", split_axis=3, concat_axis=2, tiled=True)
    epi_slope = (second_grad.astype(jnp.float32) * silu_slope(block_out)).astype(jnp.bfloat16)
    epi_grad = weight_grad(epi_slope, padded_block, 2, views_all, breadth)
    slope_pad = jnp.pad(epi_slope, ((0, 0), (0, 0), (1, 1), (0, 0), (0, 0), (1, 1)))
    first_grad = (
        second_grad.astype(jnp.float32) + epi_back(slope_pad, epi_weight, views_all, breadth)
    ).astype(jnp.bfloat16)
    first_views = lax.all_to_all(first_grad, "ang", split_axis=2, concat_axis=3, tiled=True)
    upscaled = lifted_views.reshape(
        batch_here, angular_rows, views_here, rows_here, SCALE, SCALE, breadth
    )
    upscaled = upscaled.transpose(0, 1, 2, 3, 4, 6, 5).reshape(
        batch_here, angular_rows, views_here, rows_here * SCALE, breadth * SCALE
    )
    spatial_slope = (first_views.astype(jnp.float32) * silu_slope(spatial_out)).astype(jnp.bfloat16)
    spatial_grad = weight_grad(spatial_slope, spatial_in, 3, rows_here, breadth)
    spatial_grad, epi_grad, up_grad = sum_everywhere((spatial_grad, epi_grad, up_grad))
    return (upscaled, spatial_grad, epi_grad, up_grad)


def solution(mesh):
    placed = (
        P("dp", None, "ang", "rows", None, None),
        P(),
        P(),
        P(),
        P("dp", None, "ang", "rows", None),
    )
    return jax.shard_map(
        on_device,
        mesh=mesh,
        in_specs=placed,
        out_specs=(P("dp", None, "ang", "rows", None), P(), P(), P()),
        check_vma=False,
    )
```

```python
import jax
import jax.numpy as jnp
from jax import lax
from jax.experimental import pallas as pl
from jax.experimental.pallas import tpu as pltpu
from jax.sharding import PartitionSpec as P

F32 = jnp.float32
BF16 = jnp.bfloat16
VMEM_LIMIT = 56 * 1024 * 1024


def mesh_pairs(kind, step):
    if kind == "x":
        return "rows", [(g * 4 + i, g * 4 + (i + step) % 4) for g in range(4) for i in range(4)]
    if kind == "z":
        return "rows", [(4 * i + g, 4 * ((i + step) % 4) + g) for g in range(4) for i in range(4)]
    return kind, [(i, (i + step) % 4) for i in range(4)]


def shifted(value, kind, step):
    axis, pairs = mesh_pairs(kind, step)
    return lax.ppermute(value, axis, pairs)


def gather_sum(value, kind):
    one, two, three = (shifted(value, kind, step) for step in (1, 2, 3))
    return (value + two) + (one + three)


def scatter_sum(value, kind):
    place = lax.axis_index(kind)
    mine = lax.dynamic_index_in_dim(value, place, 0, keepdims=False)
    one, two, three = (
        shifted(lax.dynamic_index_in_dim(value, (place + step) % 4, 0, keepdims=False), kind, step)
        for step in (1, 2, 3)
    )
    return (mine + two) + (one + three)


def gather_parts(value, kind):
    place = lax.axis_index(kind)
    around = jnp.stack([value] + [shifted(value, kind, step) for step in (1, 2, 3)])
    return jnp.concatenate(
        [lax.dynamic_index_in_dim(around, (place - part) % 4, 0) for part in range(4)], axis=0
    )


def sum_everywhere(flat):
    rows = flat.shape[0]
    mine = scatter_sum(flat.reshape(4, rows // 4, 128), "dp")
    for kind in ("x", "z", "ang"):
        mine = gather_sum(mine, kind)
    return gather_parts(mine, "dp").reshape(rows, 128)


def from_both(head, tail, axis):
    ends = lax.axis_size(axis) - 1
    before = lax.ppermute(tail, axis, [(i, i + 1) for i in range(ends)])
    after = lax.ppermute(head, axis, [(i + 1, i) for i in range(ends)])
    return before, after


def column(shape):
    return lax.broadcasted_iota(jnp.int32, shape, len(shape) - 1)


def from_left(values):
    return jnp.where(column(values.shape) == 0, 0.0, pltpu.roll(values, 1, axis=1))


def from_right(values):
    width = values.shape[1]
    return jnp.where(column(values.shape) == width - 1, 0.0, pltpu.roll(values, width - 1, axis=1))


def product(left, right):
    return jnp.dot(left, right, preferred_element_type=F32)


def product_nt(left, right):
    return lax.dot_general(left, right, (((1,), (1,)), ((), ())), preferred_element_type=F32)


def silu_slope(values, gate):
    return gate * (1.0 + values * (1.0 - gate))


def taps_of(slope):
    return jnp.concatenate(
        [from_right(slope).astype(BF16), slope.astype(BF16), from_left(slope).astype(BF16)], axis=0
    )


def deal_kernel(own_ref, before_ref, after_ref, dealt_ref, deal_ref):
    size = deal_ref.shape[0]
    source = lax.broadcasted_iota(jnp.int32, (size, size), 0)
    target = lax.broadcasted_iota(jnp.int32, (size, size), 1)
    lanes = size // 4
    wanted = 4 * (target % lanes) + target // lanes
    deal = jnp.where(source == wanted, 1.0, 0.0).astype(BF16)
    deal_ref[...] = deal
    views = [before_ref[...], own_ref[0], own_ref[1], after_ref[...]]
    for block in range(own_ref.shape[2] // size):
        stacked = jnp.concatenate([v[:, block * size : (block + 1) * size] for v in views], axis=0)
        moved = product(stacked, deal).astype(BF16)
        for view in range(4):
            for q in range(4):
                dealt_ref[view, q * 16 : (q + 1) * 16, block * lanes : (block + 1) * lanes] = moved[
                    view * 16 : (view + 1) * 16, q * lanes : (q + 1) * lanes
                ]


def spatial_kernel(light_ref, above_ref, below_ref, weight_ref, first_ref, out_ref):
    rows = light_ref.shape[1]
    lines = [above_ref[0, 0]] + [light_ref[0, h] for h in range(rows)] + [below_ref[0, 0]]
    chans = lines[0].shape[0]
    for h in range(rows):
        stacked = jnp.concatenate(lines[h : h + 3], axis=0)
        taps = product(weight_ref[...], stacked)
        total = (
            taps[chans : 2 * chans]
            + from_left(taps[:chans])
            + from_right(taps[2 * chans :])
        )
        out_ref[0, h] = total
        first_ref[0, h] = (lines[h + 1].astype(F32) + total * jax.nn.sigmoid(total)).astype(BF16)


def main_kernel(
    own_ref,
    before_ref,
    after_ref,
    dealt_ref,
    deal_ref,
    light_ref,
    above_ref,
    below_ref,
    out_ref,
    epi_ref,
    back_ref,
    lift_ref,
    drop_ref,
    up_ref,
    pay_ref,
    lines,
    epi_acc,
    spatial_acc,
    up_acc,
    lift_acc,
):
    step = pl.program_id(0)
    rows = light_ref.shape[1]
    chans = light_ref.shape[2]

    @pl.when(step == 0)
    def _():
        for v in range(2):
            lines[v, :chans] = above_ref[v, 0]
            for h in range(rows):
                lines[v, (h + 1) * chans : (h + 2) * chans] = light_ref[v, h]
            lines[v, (rows + 1) * chans :] = below_ref[v, 0]
        epi_acc[...] = jnp.zeros_like(epi_acc)
        spatial_acc[...] = jnp.zeros_like(spatial_acc)
        up_acc[...] = jnp.zeros_like(up_acc)
        lift_acc[...] = jnp.zeros_like(lift_acc)

    firsts = jnp.concatenate(
        [ref[v, 0] for ref in (before_ref, own_ref, after_ref) for v in range(2)], axis=0
    )
    here = (lax.broadcasted_iota(jnp.int32, (4 * 16, chans), 0) % 16) // 4 == step
    grads, slopes, slopes_f = [], [], []
    for v in range(4):
        window = firsts[v * chans : (v + 3) * chans]
        taps = product(epi_ref[...], window)
        total = (
            taps[chans : 2 * chans]
            + from_left(taps[:chans])
            + from_right(taps[2 * chans :])
        )
        gate = jax.nn.sigmoid(total)
        grad = product(drop_ref[0], dealt_ref[v]).astype(BF16).astype(F32)
        slope = grad * silu_slope(total, gate)
        slopes.append(slope.astype(BF16))
        if v in (1, 2):
            grads.append(grad)
            second = (own_ref[v - 1, 0].astype(F32) + total * gate).astype(BF16)
            lift_acc[v - 1] += product(lift_ref[0], second)
            up_acc[...] += jnp.where(here, product_nt(dealt_ref[v], second), 0.0)
            epi_acc[...] += product_nt(taps_of(slope), window)
    slopes = jnp.concatenate(slopes, axis=0)
    for v in range(2):
        taps = product(back_ref[...], slopes[v * chans : (v + 3) * chans])
        first_grad = grads[v] + (
            taps[chans : 2 * chans]
            + from_right(taps[:chans])
            + from_left(taps[2 * chans :])
        )
        first_grad = first_grad.astype(BF16).astype(F32)
        total = out_ref[v, 0]
        slope = first_grad * silu_slope(total, jax.nn.sigmoid(total))
        near = lines[v, pl.ds(pl.multiple_of(step * chans, chans), 3 * chans)]
        spatial_acc[...] += product_nt(taps_of(slope), near)

    @pl.when(step == pl.num_programs(0) - 1)
    def _():
        size = deal_ref.shape[0]
        lanes = size // 4
        lifted = [lift_acc[v].astype(BF16) for v in range(2)]
        for block in range(up_ref.shape[2] // size):
            spread = jnp.concatenate(
                [
                    jnp.concatenate(
                        [
                            lifted[v][q * 16 : (q + 1) * 16, block * lanes : (block + 1) * lanes]
                            for q in range(4)
                        ],
                        axis=1,
                    )
                    for v in range(2)
                ],
                axis=0,
            )
            woven = product_nt(spread, deal_ref[...]).astype(BF16)
            for v in range(2):
                up_ref[v, :, block * size : (block + 1) * size] = woven[v * 16 : (v + 1) * 16]
        three = 3 * chans
        pay_ref[:three] = spatial_acc[:, :128]
        pay_ref[three : 2 * three] = epi_acc[:, :128]
        pay_ref[2 * three : 3 * three] = jnp.concatenate(
            [spatial_acc[:, 128:], epi_acc[:, 128:]], axis=1
        )
        pay_ref[3 * three :] = jnp.concatenate([up_acc[...], jnp.zeros_like(up_acc)], axis=1)


def unpack_kernel(pay_ref, spatial_ref, epi_ref, up_ref):
    chans = spatial_ref.shape[2]
    three = 3 * chans
    for which, ref in enumerate((spatial_ref, epi_ref)):
        for j in range(3):
            both = pay_ref[which * three + j * chans : which * three + (j + 1) * chans, :]
            ref[0, j] = both[:, :chans]
            ref[1, j] = both[:, chans:]
            last = pay_ref[2 * three + j * chans : 2 * three + (j + 1) * chans, :]
            ref[2, j] = last[:, which * chans : (which + 1) * chans]
    for p in range(4):
        for q in range(4):
            base = 3 * three + q * 16 + p
            total = pay_ref[base : base + 1, :chans]
            for h in range(1, 4):
                total = total + pay_ref[base + 4 * h : base + 4 * h + 1, :chans]
            up_ref[4 * p + q : 4 * p + q + 1, :] = total


def whole(shape):
    return pl.BlockSpec(shape, lambda *_: (0,) * len(shape))


def on_device(light_field, spatial_weight, epi_weight, upsample_weight, image_grad):
    _, _, views, rows, chans, breadth = light_field.shape
    light = light_field.reshape(views, rows, chans, breadth)
    image = image_grad.reshape(views, image_grad.shape[3], image_grad.shape[4])
    params = pltpu.CompilerParams(vmem_limit_bytes=VMEM_LIMIT)

    above, below = from_both(light[:, :1], light[:, rows - 1 :], "rows")
    image_before, image_after = from_both(image[0], image[views - 1], "ang")

    three = 3 * chans
    spatial_taps = spatial_weight.transpose(1, 2, 0, 3).reshape(three, three)
    epi_taps = epi_weight.transpose(1, 2, 0, 3).reshape(three, three)
    back_taps = epi_weight[::-1].transpose(1, 3, 0, 2).reshape(three, three)
    by_q = upsample_weight.reshape(4, 4, chans).transpose(1, 0, 2)
    same = jnp.eye(rows, dtype=BF16)
    lift = (same[:, None, :, None, None] * by_q[None, :, None, :, :]).reshape(rows, 64, chans)
    drop = lift.transpose(0, 2, 1)

    dealt, deal = pl.pallas_call(
        deal_kernel,
        out_shape=(
            jax.ShapeDtypeStruct((4, 64, breadth), BF16),
            jax.ShapeDtypeStruct((512, 512), BF16),
        ),
        compiler_params=params,
        name="deal",
    )(image, image_before, image_after)

    by_view = pl.BlockSpec((1, rows, chans, breadth), lambda v: (v, 0, 0, 0))
    edge = pl.BlockSpec((1, 1, chans, breadth), lambda v: (v, 0, 0, 0))
    first, spatial_out = pl.pallas_call(
        spatial_kernel,
        grid=(views,),
        in_specs=[by_view, edge, edge, whole((three, three))],
        out_specs=(by_view, by_view),
        out_shape=(
            jax.ShapeDtypeStruct(light.shape, BF16),
            jax.ShapeDtypeStruct(light.shape, F32),
        ),
        compiler_params=params,
        name="spatial",
    )(light, above, below, spatial_taps)

    before, after = from_both(first, first, "ang")

    by_row = pl.BlockSpec((views, 1, chans, breadth), lambda h: (0, h, 0, 0))
    up, pay = pl.pallas_call(
        main_kernel,
        grid=(rows,),
        in_specs=[
            by_row,
            by_row,
            by_row,
            whole(dealt.shape),
            whole(deal.shape),
            whole(light.shape),
            whole(above.shape),
            whole(below.shape),
            by_row,
            whole((three, three)),
            whole((three, three)),
            pl.BlockSpec((1, 64, chans), lambda h: (h, 0, 0)),
            pl.BlockSpec((1, chans, 64), lambda h: (h, 0, 0)),
        ],
        out_specs=(whole(image.shape), whole((640, 128))),
        out_shape=(
            jax.ShapeDtypeStruct(image.shape, BF16),
            jax.ShapeDtypeStruct((640, 128), F32),
        ),
        scratch_shapes=[
            pltpu.VMEM((views, (rows + 2) * chans, breadth), BF16),
            pltpu.VMEM((three, three), F32),
            pltpu.VMEM((three, three), F32),
            pltpu.VMEM((64, chans), F32),
            pltpu.VMEM((views, 64, breadth), F32),
        ],
        compiler_params=params,
        name="main",
    )(
        first,
        before,
        after,
        dealt,
        deal,
        light,
        above,
        below,
        spatial_out,
        epi_taps,
        back_taps,
        lift,
        drop,
    )

    total = sum_everywhere(pay)
    spatial_grad, epi_grad, up_grad = pl.pallas_call(
        unpack_kernel,
        out_shape=(
            jax.ShapeDtypeStruct(spatial_weight.shape, F32),
            jax.ShapeDtypeStruct(epi_weight.shape, F32),
            jax.ShapeDtypeStruct(upsample_weight.shape, F32),
        ),
        compiler_params=params,
        name="unpack",
    )(total)
    return (up.reshape(image_grad.shape), spatial_grad, epi_grad, up_grad)


def solution(mesh):
    placed = (
        P("dp", None, "ang", "rows", None, None),
        P(),
        P(),
        P(),
        P("dp", None, "ang", "rows", None),
    )
    return jax.shard_map(
        on_device,
        mesh=mesh,
        in_specs=placed,
        out_specs=(P("dp", None, "ang", "rows", None), P(), P(), P()),
        check_vma=False,
    )
```

```python
import jax
import jax.numpy as jnp
from jax import lax
from jax.experimental import pallas as pl
from jax.experimental.pallas import tpu as pltpu
from jax.sharding import Mesh
from jax.sharding import PartitionSpec as P

F32 = jnp.float32
BF16 = jnp.bfloat16
DP = ("pair", "core")
ROWS = ("quad", "x")
VMEM_LIMIT = 40 * 1024 * 1024


def swapped(value, axis, step):
    count = lax.axis_size(axis)
    return lax.ppermute(value, axis, [(i, (i + step) % count) for i in range(count)])


def sum_everywhere(pay):
    plane = ("ang", "x")
    rows = pay.shape[0]
    mine = lax.all_to_all(
        pay.reshape(16, rows // 16, 128), plane, split_axis=0, concat_axis=0, tiled=True
    ).sum(0)
    for axis in ("core", "pair"):
        mine = mine + swapped(mine, axis, 1)
    one, two, three = (swapped(mine, "quad", step) for step in (1, 2, 3))
    mine = (mine + two) + (one + three)
    spread = jnp.broadcast_to(mine[None], (16,) + mine.shape)
    return lax.all_to_all(spread, plane, split_axis=0, concat_axis=0, tiled=True).reshape(rows, 128)


def from_both(head, tail, axis):
    count = lax.axis_size(axis)
    before = lax.ppermute(tail, axis, [(i, (i + 1) % count) for i in range(count)])
    after = lax.ppermute(head, axis, [((i + 1) % count, i) for i in range(count)])
    return before, after


def has_neighbours(axis, count):
    place = lax.axis_index(axis)
    return place > 0, place < count - 1


def kept(flag, values):
    return jnp.where(flag, values, jnp.zeros_like(values))


def column(shape):
    return lax.broadcasted_iota(jnp.int32, shape, len(shape) - 1)


def from_left(values):
    return jnp.where(column(values.shape) == 0, 0.0, pltpu.roll(values, 1, axis=1))


def from_right(values):
    width = values.shape[1]
    return jnp.where(column(values.shape) == width - 1, 0.0, pltpu.roll(values, width - 1, axis=1))


def product(left, right):
    return jnp.dot(left, right, preferred_element_type=F32)


def product_nt(left, right):
    return lax.dot_general(left, right, (((1,), (1,)), ((), ())), preferred_element_type=F32)


def gate_of(values):
    return 0.5 * jnp.tanh(0.5 * values) + 0.5


def silu_slope(values, gate):
    return gate * (1.0 + values * (1.0 - gate))


def taps_of(slope):
    return jnp.concatenate(
        [from_right(slope).astype(BF16), slope.astype(BF16), from_left(slope).astype(BF16)], axis=0
    )


def conv_taps(weights, stacked, forward):
    taps = product(weights, stacked)
    chans = weights.shape[0] // 3
    left, right = (from_left, from_right) if forward else (from_right, from_left)
    return taps[chans : 2 * chans] + left(taps[:chans]) + right(taps[2 * chans :])


def unit(size):
    return jnp.where(
        lax.broadcasted_iota(jnp.int32, (size, size), 0)
        == lax.broadcasted_iota(jnp.int32, (size, size), 1),
        1.0,
        0.0,
    ).astype(BF16)


def forward_taps(ref, taps_ref):
    chans = ref.shape[2]
    for j in range(3):
        taps_ref[j * chans : (j + 1) * chans] = jnp.concatenate([ref[i, j] for i in range(3)], axis=1)


def prepare_weights(spatial_ref, epi_ref, up_ref, taps_ref, epi_taps_ref, back_ref, lift_ref, drop_ref):
    chans = spatial_ref.shape[2]
    forward_taps(spatial_ref, taps_ref)
    forward_taps(epi_ref, epi_taps_ref)
    stacked = jnp.concatenate(
        [jnp.concatenate([epi_ref[2 - s, j] for j in range(3)], axis=1) for s in range(3)], axis=0
    )
    back_ref[...] = product_nt(unit(3 * chans), stacked).astype(BF16)
    turned = product_nt(unit(chans), up_ref[...]).astype(BF16)
    line = lax.broadcasted_iota(jnp.int32, (64, 16), 0)
    sub = lax.broadcasted_iota(jnp.int32, (64, 16), 1)
    match = sub == 4 * (line % 4) + line // 16
    for h in range(4):
        pick = jnp.where(match & ((line % 16) // 4 == h), 1.0, 0.0).astype(BF16)
        lift_ref[h] = product(pick, up_ref[...]).astype(BF16)
        drop_ref[h] = product_nt(turned, pick).astype(BF16)


def inner_kernel(
    image_ref,
    light_ref,
    spatial_ref,
    epi_ref,
    up_ref,
    mixed_ref,
    out_ref,
    deal_ref,
    weight_ref,
    epi_taps_ref,
    back_ref,
    lift_ref,
    drop_ref,
):
    prepare_weights(
        spatial_ref, epi_ref, up_ref, weight_ref, epi_taps_ref, back_ref, lift_ref, drop_ref
    )
    size = deal_ref.shape[0]
    source = lax.broadcasted_iota(jnp.int32, (size, size), 0)
    target = lax.broadcasted_iota(jnp.int32, (size, size), 1)
    lanes = size // 4
    wanted = 4 * (target % lanes) + target // lanes
    deal = jnp.where(source == wanted, 1.0, 0.0).astype(BF16)
    deal_ref[...] = deal
    chans = light_ref.shape[2]
    for block in range(image_ref.shape[2] // size):
        cut = slice(block * size, (block + 1) * size)
        stacked = jnp.concatenate([image_ref[0, :, cut], image_ref[1, :, cut]], axis=0)
        moved = product(stacked, deal).astype(BF16)
        for view in range(2):
            for q in range(4):
                mixed_ref[
                    view,
                    2 * chans + q * 16 : 2 * chans + (q + 1) * 16,
                    block * lanes : (block + 1) * lanes,
                ] = moved[view * 16 : (view + 1) * 16, q * lanes : (q + 1) * lanes]
    for view in range(2):
        for slot, h in enumerate((1, 2)):
            stacked = jnp.concatenate([light_ref[view, h + k] for k in (-1, 0, 1)], axis=0)
            total = conv_taps(weight_ref[...], stacked, True)
            out_ref[view, slot] = total
            first = light_ref[view, h].astype(F32) + total * gate_of(total)
            mixed_ref[view, slot * chans : (slot + 1) * chans] = first.astype(BF16)


def edge_kernel(light_ref, above_ref, below_ref, weight_ref, first_ref, out_ref):
    chans = light_ref.shape[2]
    has_above, has_below = has_neighbours(ROWS, 16)
    for view in range(2):
        for slot, h in enumerate((0, 3)):
            if slot == 0:
                stacked = [kept(has_above, above_ref[view, 0]), light_ref[view, 0], light_ref[view, 1]]
            else:
                stacked = [light_ref[view, 2], light_ref[view, 3], kept(has_below, below_ref[view, 0])]
            total = conv_taps(weight_ref[...], jnp.concatenate(stacked, axis=0), True)
            out_ref[view, slot] = total
            first = light_ref[view, h].astype(F32) + total * gate_of(total)
            first_ref[view, slot * chans : (slot + 1) * chans] = first.astype(BF16)


def main_rows(rows, firsts, dealt, near, out_ref, epi_ref, back_ref, lift_ref, drop_ref, pay_ref, lift_out):
    chans = drop_ref.shape[1]
    three = 3 * chans
    lifted = [None, None]
    up_total = None
    epi_left, epi_right, spatial_left, spatial_right = [], [], [], []
    has_before, has_after = has_neighbours("ang", 4)
    for slot, h in enumerate(rows):
        cut = slice(slot * chans, (slot + 1) * chans)
        stack = jnp.concatenate(
            [kept(has_before, firsts[0][v, cut]) for v in range(2)]
            + [firsts[1][v, cut] for v in range(2)]
            + [kept(has_after, firsts[2][v, cut]) for v in range(2)],
            axis=0,
        )
        here = (lax.broadcasted_iota(jnp.int32, (64, chans), 0) % 16) // 4 == h
        grads, slopes = [], []
        for v in range(4):
            window = stack[v * chans : (v + 3) * chans]
            total = conv_taps(epi_ref[...], window, True)
            gate = gate_of(total)
            grad = product(drop_ref[h], dealt[v]).astype(BF16).astype(F32)
            slope = grad * silu_slope(total, gate)
            slopes.append(slope.astype(BF16))
            if v in (1, 2):
                grads.append(grad)
                own = stack[(v + 1) * chans : (v + 2) * chans]
                second = (own.astype(F32) + total * gate).astype(BF16)
                part = product(lift_ref[h], second)
                lifted[v - 1] = part if slot == 0 else lifted[v - 1] + part
                part = jnp.where(here, product_nt(dealt[v], second), 0.0)
                up_total = part if up_total is None else up_total + part
                epi_left.append(taps_of(slope))
                epi_right.append(window)
        slopes = jnp.concatenate(slopes, axis=0)
        for v in range(2):
            moved = conv_taps(back_ref[...], slopes[v * chans : (v + 3) * chans], False)
            first_grad = (grads[v] + moved).astype(BF16).astype(F32)
            total = out_ref[v, slot]
            slope = first_grad * silu_slope(total, gate_of(total))
            spatial_left.append(taps_of(slope))
            spatial_right.append(jnp.concatenate(near(v, h), axis=0))
    for v in range(2):
        lift_out[v] = lifted[v].astype(BF16)
    epi = product_nt(jnp.concatenate(epi_left, axis=1), jnp.concatenate(epi_right, axis=1))
    spatial = product_nt(
        jnp.concatenate(spatial_left, axis=1), jnp.concatenate(spatial_right, axis=1)
    )
    pieces = (
        spatial[:, :128],
        epi[:, :128],
        jnp.concatenate([spatial[:, 128:], epi[:, 128:]], axis=1),
        jnp.concatenate([up_total, jnp.zeros_like(up_total)], axis=1),
    )
    start = 0
    for piece in pieces:
        end = start + piece.shape[0]
        pay_ref[start:end] = piece
        start = end


def dealt_views(own_ref, before_ref, after_ref, chans):
    has_before, has_after = has_neighbours("ang", 4)
    return [
        kept(has_before, before_ref[1, 2 * chans :]),
        own_ref[0, 2 * chans :],
        own_ref[1, 2 * chans :],
        kept(has_after, after_ref[0, 2 * chans :]),
    ]


def main_inner_kernel(
    own_ref, before_ref, after_ref, light_ref, out_ref, epi_ref, back_ref, lift_ref, drop_ref, pay_ref, lift_out
):
    def near(v, h):
        return [light_ref[v, h + k] for k in (-1, 0, 1)]

    main_rows(
        (1, 2),
        (before_ref, own_ref, after_ref),
        dealt_views(own_ref, before_ref, after_ref, light_ref.shape[2]),
        near,
        out_ref,
        epi_ref,
        back_ref,
        lift_ref,
        drop_ref,
        pay_ref,
        lift_out,
    )


def main_edge_kernel(
    first_ref,
    first_before_ref,
    first_after_ref,
    own_ref,
    before_ref,
    after_ref,
    light_ref,
    above_ref,
    below_ref,
    out_ref,
    epi_ref,
    back_ref,
    lift_ref,
    drop_ref,
    inner_pay_ref,
    pay_ref,
    lift_out,
):
    has_above, has_below = has_neighbours(ROWS, 16)

    def near(v, h):
        if h == 0:
            return [kept(has_above, above_ref[v, 0]), light_ref[v, 0], light_ref[v, 1]]
        return [light_ref[v, 2], light_ref[v, 3], kept(has_below, below_ref[v, 0])]

    main_rows(
        (0, 3),
        (first_before_ref, first_ref, first_after_ref),
        dealt_views(own_ref, before_ref, after_ref, light_ref.shape[2]),
        near,
        out_ref,
        epi_ref,
        back_ref,
        lift_ref,
        drop_ref,
        pay_ref,
        lift_out,
    )
    pay_ref[...] += inner_pay_ref[...]


def weave_kernel(inner_ref, edge_ref, deal_ref, up_ref):
    size = deal_ref.shape[0]
    lanes = size // 4
    lifted = [inner_ref[v] + edge_ref[v] for v in range(2)]
    for block in range(up_ref.shape[2] // size):
        spread = [
            jnp.concatenate(
                [
                    lifted[v][q * 16 : (q + 1) * 16, block * lanes : (block + 1) * lanes]
                    for q in range(4)
                ],
                axis=1,
            )
            for v in range(2)
        ]
        woven = product_nt(jnp.concatenate(spread, axis=0), deal_ref[...]).astype(BF16)
        for v in range(2):
            up_ref[v, :, block * size : (block + 1) * size] = woven[v * 16 : (v + 1) * 16]


def unpack_kernel(pay_ref, spatial_ref, epi_ref, up_ref):
    chans = spatial_ref.shape[2]
    three = 3 * chans
    for which, ref in enumerate((spatial_ref, epi_ref)):
        for j in range(3):
            both = pay_ref[which * three + j * chans : which * three + (j + 1) * chans, :]
            ref[0, j] = both[:, :chans]
            ref[1, j] = both[:, chans:]
            last = pay_ref[2 * three + j * chans : 2 * three + (j + 1) * chans, :]
            ref[2, j] = last[:, which * chans : (which + 1) * chans]
    for p in range(4):
        for q in range(4):
            base = 3 * three + q * 16 + p
            total = pay_ref[base : base + 1, :chans]
            for h in range(1, 4):
                total = total + pay_ref[base + 4 * h : base + 4 * h + 1, :chans]
            up_ref[4 * p + q : 4 * p + q + 1, :] = total


def local_call(kernel, shapes, name, *operands, micros=3):
    return pl.pallas_call(
        kernel,
        out_shape=shapes,
        cost_estimate=pl.CostEstimate(
            flops=micros * 1_000_000_000, bytes_accessed=micros * 3_000_000, transcendentals=0
        ),
        compiler_params=pltpu.CompilerParams(vmem_limit_bytes=VMEM_LIMIT),
        name=name,
    )(*(pltpu.with_memory_space_constraint(operand, pltpu.VMEM) for operand in operands))


def on_device(light_field, spatial_weight, epi_weight, upsample_weight, image_grad):
    _, _, views, rows, chans, breadth = light_field.shape
    light = light_field.reshape(views, rows, chans, breadth)
    image = image_grad.reshape(views, image_grad.shape[3], image_grad.shape[4])

    above, below = from_both(light[:, :1], light[:, rows - 1 :], ROWS)

    three = 3 * chans
    like = pltpu.VMEM
    plain = jax.ShapeDtypeStruct
    half_out = like((views, 2, chans, breadth), F32)
    taps = like((three, three), BF16)
    mixed, inner_out, deal, spatial_taps, epi_taps, back_taps, lift, drop = local_call(
        inner_kernel,
        (
            like((views, 2 * chans + 64, breadth), BF16),
            half_out,
            like((512, 512), BF16),
            taps,
            taps,
            taps,
            like((rows, 64, chans), BF16),
            like((rows, chans, 64), BF16),
        ),
        "inner",
        image,
        light,
        spatial_weight,
        epi_weight,
        upsample_weight,
    )
    mixed_before, mixed_after = from_both(mixed, mixed, "ang")
    first, edge_out = local_call(
        edge_kernel,
        (like((views, 2 * chans, breadth), BF16), half_out),
        "edge",
        light,
        above,
        below,
        spatial_taps,
    )
    first_before, first_after = from_both(first, first, "ang")

    weights = (epi_taps, back_taps, lift, drop)
    lift_half = like((views, 64, breadth), BF16)
    whole_pay = like((640, 128), F32)
    inner_pay, inner_lift = local_call(
        main_inner_kernel,
        (whole_pay, lift_half),
        "main_inner",
        mixed,
        mixed_before,
        mixed_after,
        light,
        inner_out,
        *weights,
    )
    pay, edge_lift = local_call(
        main_edge_kernel,
        (whole_pay, lift_half),
        "main_edge",
        first,
        first_before,
        first_after,
        mixed,
        mixed_before,
        mixed_after,
        light,
        above,
        below,
        edge_out,
        *weights,
        inner_pay,
    )
    up = local_call(
        weave_kernel, plain(image.shape, BF16), "weave", inner_lift, edge_lift, deal
    )
    spatial_grad, epi_grad, up_grad = local_call(
        unpack_kernel,
        (
            plain(spatial_weight.shape, F32),
            plain(epi_weight.shape, F32),
            plain(upsample_weight.shape, F32),
        ),
        "unpack",
        sum_everywhere(pay),
    )
    return (up.reshape(image_grad.shape), spatial_grad, epi_grad, up_grad)


def solution(mesh):
    split = Mesh(mesh.devices.reshape(2, 2, 4, 4, 4), ("pair", "core", "ang", "quad", "x"))
    image_spec = P(DP, None, "ang", ROWS, None)
    return jax.shard_map(
        on_device,
        mesh=split,
        in_specs=(P(DP, None, "ang", ROWS, None, None), P(), P(), P(), image_spec),
        out_specs=(image_spec, P(), P(), P()),
        check_vma=False,
    )
```

```python
import jax
import jax.numpy as jnp
from jax import lax
from jax.experimental import pallas as pl
from jax.experimental.pallas import tpu as pltpu
from jax.sharding import Mesh
from jax.sharding import PartitionSpec as P

F32 = jnp.float32
BF16 = jnp.bfloat16
DP = ("pair", "core")
ROWS = ("quad", "x")
VMEM_LIMIT = 40 * 1024 * 1024


def swapped(value, axis, step):
    count = lax.axis_size(axis)
    return lax.ppermute(value, axis, [(i, (i + step) % count) for i in range(count)])


def sum_everywhere(pay):
    plane = ("ang", "x")
    rows = pay.shape[0]
    mine = lax.all_to_all(
        pay.reshape(16, rows // 16, 128), plane, split_axis=0, concat_axis=0, tiled=True
    ).sum(0)
    for axis in ("core", "pair"):
        mine = mine + swapped(mine, axis, 1)
    for flip in (1, 3):
        mine = mine + lax.ppermute(mine, "quad", [(i, i ^ flip) for i in range(4)])
    spread = jnp.broadcast_to(mine.astype(BF16)[None], (16,) + mine.shape)
    return lax.all_to_all(spread, plane, split_axis=0, concat_axis=0, tiled=True).reshape(rows, 128)


def is_even(axis):
    return lax.axis_index(axis) % 2 == 0


def with_next_and_before(first_send, second_send, axis):
    count = lax.axis_size(axis)
    odd = [(i, (i + 1) % count) for i in range(1, count, 2)]
    two = lax.ppermute(second_send, axis, odd + [(j, i) for i, j in odd])
    one = lax.ppermute(first_send, axis, [(i, i ^ 1) for i in range(count)])
    return one, two


def has_neighbours(axis, count):
    place = lax.axis_index(axis)
    return place > 0, place < count - 1


def chosen(flags, one, two):
    even, present = flags
    values = jnp.where(even, one, two)
    return jnp.where(present, values, jnp.zeros_like(values))


def sides(axis, count):
    even = is_even(axis)
    before, after = has_neighbours(axis, count)
    return (jnp.logical_not(even), before), (even, after)


def column(shape):
    return lax.broadcasted_iota(jnp.int32, shape, len(shape) - 1)


def from_left(values):
    return jnp.where(column(values.shape) == 0, 0.0, pltpu.roll(values, 1, axis=1))


def from_right(values):
    width = values.shape[1]
    return jnp.where(column(values.shape) == width - 1, 0.0, pltpu.roll(values, width - 1, axis=1))


def product(left, right):
    return jnp.dot(left, right, preferred_element_type=F32)


def product_nt(left, right):
    return lax.dot_general(left, right, (((1,), (1,)), ((), ())), preferred_element_type=F32)


def gate_of(values):
    return 0.5 * jnp.tanh(0.5 * values) + 0.5


def silu_slope(values, gate):
    return gate * (1.0 + values * (1.0 - gate))


def taps_of(slope):
    return jnp.concatenate(
        [from_right(slope).astype(BF16), slope.astype(BF16), from_left(slope).astype(BF16)], axis=0
    )


def conv_taps(weights, stacked, forward):
    taps = product(weights, stacked)
    chans = weights.shape[0] // 3
    left, right = (from_left, from_right) if forward else (from_right, from_left)
    return taps[chans : 2 * chans] + left(taps[:chans]) + right(taps[2 * chans :])


def unit(size):
    return jnp.where(
        lax.broadcasted_iota(jnp.int32, (size, size), 0)
        == lax.broadcasted_iota(jnp.int32, (size, size), 1),
        1.0,
        0.0,
    ).astype(BF16)


def forward_taps(ref, taps_ref):
    chans = ref.shape[2]
    for j in range(3):
        taps_ref[j * chans : (j + 1) * chans] = jnp.concatenate([ref[i, j] for i in range(3)], axis=1)


def prepare_weights(spatial_ref, epi_ref, up_ref, taps_ref, epi_taps_ref, back_ref, lift_ref, drop_ref):
    chans = spatial_ref.shape[2]
    forward_taps(spatial_ref, taps_ref)
    forward_taps(epi_ref, epi_taps_ref)
    stacked = jnp.concatenate(
        [jnp.concatenate([epi_ref[2 - s, j] for j in range(3)], axis=1) for s in range(3)], axis=0
    )
    back_ref[...] = product_nt(unit(3 * chans), stacked).astype(BF16)
    turned = product_nt(unit(chans), up_ref[...]).astype(BF16)
    line = lax.broadcasted_iota(jnp.int32, (64, 16), 0)
    sub = lax.broadcasted_iota(jnp.int32, (64, 16), 1)
    match = sub == 4 * (line % 4) + line // 16
    for h in range(4):
        pick = jnp.where(match & ((line % 16) // 4 == h), 1.0, 0.0).astype(BF16)
        lift_ref[h] = product(pick, up_ref[...]).astype(BF16)
        drop_ref[h] = product_nt(turned, pick).astype(BF16)


def inner_kernel(
    image_hbm,
    light_hbm,
    spatial_hbm,
    epi_hbm,
    up_hbm,
    mixed_ref,
    out_ref,
    deal_ref,
    weight_ref,
    epi_taps_ref,
    back_ref,
    lift_ref,
    drop_ref,
    light_ref,
    one_ref,
    two_ref,
    image_ref,
    spatial_ref,
    epi_ref,
    up_ref,
    sems,
):
    pairs = (
        (spatial_hbm, spatial_ref),
        (image_hbm, image_ref),
        (light_hbm, light_ref),
        (epi_hbm, epi_ref),
        (up_hbm, up_ref),
    )
    copies = [
        pltpu.make_async_copy(source, target, sems.at[place])
        for place, (source, target) in enumerate(pairs)
    ]
    for copy in copies:
        copy.start()
    size = deal_ref.shape[0]
    source = lax.broadcasted_iota(jnp.int32, (size, size), 0)
    target = lax.broadcasted_iota(jnp.int32, (size, size), 1)
    lanes = size // 4
    wanted = 4 * (target % lanes) + target // lanes
    deal = jnp.where(source == wanted, 1.0, 0.0).astype(BF16)
    deal_ref[...] = deal
    chans = light_ref.shape[2]
    for copy in copies:
        copy.wait()
    even = is_even(ROWS)
    last = light_ref.shape[1] - 1
    for view in range(2):
        one_ref[view, 0] = jnp.where(even, light_ref[view, last], light_ref[view, 0])
        two_ref[view, 0] = jnp.where(even, light_ref[view, 0], light_ref[view, last])
    prepare_weights(
        spatial_ref, epi_ref, up_ref, weight_ref, epi_taps_ref, back_ref, lift_ref, drop_ref
    )
    for block in range(image_ref.shape[2] // size):
        cut = slice(block * size, (block + 1) * size)
        stacked = jnp.concatenate([image_ref[0, :, cut], image_ref[1, :, cut]], axis=0)
        moved = product(stacked, deal).astype(BF16)
        for view in range(2):
            for q in range(4):
                mixed_ref[
                    view,
                    2 * chans + q * 16 : 2 * chans + (q + 1) * 16,
                    block * lanes : (block + 1) * lanes,
                ] = moved[view * 16 : (view + 1) * 16, q * lanes : (q + 1) * lanes]
    for view in range(2):
        for slot, h in enumerate((1, 2)):
            stacked = jnp.concatenate([light_ref[view, h + k] for k in (-1, 0, 1)], axis=0)
            total = conv_taps(weight_ref[...], stacked, True)
            out_ref[view, slot] = total
            first = light_ref[view, h].astype(F32) + total * gate_of(total)
            mixed_ref[view, slot * chans : (slot + 1) * chans] = first.astype(BF16)


def edge_kernel(light_ref, one_ref, two_ref, weight_ref, first_ref, out_ref):
    chans = light_ref.shape[2]
    above, below = sides(ROWS, 16)
    for view in range(2):
        for slot, h in enumerate((0, 3)):
            if slot == 0:
                stacked = [chosen(above, one_ref[view, 0], two_ref[view, 0]), light_ref[view, 0], light_ref[view, 1]]
            else:
                stacked = [light_ref[view, 2], light_ref[view, 3], chosen(below, one_ref[view, 0], two_ref[view, 0])]
            total = conv_taps(weight_ref[...], jnp.concatenate(stacked, axis=0), True)
            out_ref[view, slot] = total
            first = light_ref[view, h].astype(F32) + total * gate_of(total)
            first_ref[view, slot * chans : (slot + 1) * chans] = first.astype(BF16)


def main_rows(rows, firsts, dealt, near, out_ref, epi_ref, back_ref, lift_ref, drop_ref, pay_ref, lift_out):
    chans = drop_ref.shape[1]
    three = 3 * chans
    lifted = [None, None]
    up_total = None
    epi_left, epi_right, spatial_left, spatial_right = [], [], [], []
    before, after = sides("ang", 4)
    for slot, h in enumerate(rows):
        cut = slice(slot * chans, (slot + 1) * chans)
        stack = jnp.concatenate(
            [chosen(before, firsts[1][v, cut], firsts[2][v, cut]) for v in range(2)]
            + [firsts[0][v, cut] for v in range(2)]
            + [chosen(after, firsts[1][v, cut], firsts[2][v, cut]) for v in range(2)],
            axis=0,
        )
        here = (lax.broadcasted_iota(jnp.int32, (64, chans), 0) % 16) // 4 == h
        grads, slopes = [], []
        for v in range(4):
            window = stack[v * chans : (v + 3) * chans]
            total = conv_taps(epi_ref[...], window, True)
            gate = gate_of(total)
            grad = product(drop_ref[h], dealt[v]).astype(BF16).astype(F32)
            slope = grad * silu_slope(total, gate)
            slopes.append(slope.astype(BF16))
            if v in (1, 2):
                grads.append(grad)
                own = stack[(v + 1) * chans : (v + 2) * chans]
                second = (own.astype(F32) + total * gate).astype(BF16)
                part = product(lift_ref[h], second)
                lifted[v - 1] = part if slot == 0 else lifted[v - 1] + part
                part = jnp.where(here, product_nt(dealt[v], second), 0.0)
                up_total = part if up_total is None else up_total + part
                epi_left.append(taps_of(slope))
                epi_right.append(window)
        slopes = jnp.concatenate(slopes, axis=0)
        for v in range(2):
            moved = conv_taps(back_ref[...], slopes[v * chans : (v + 3) * chans], False)
            first_grad = (grads[v] + moved).astype(BF16).astype(F32)
            total = out_ref[v, slot]
            slope = first_grad * silu_slope(total, gate_of(total))
            spatial_left.append(taps_of(slope))
            spatial_right.append(jnp.concatenate(near(v, h), axis=0))
    for v in range(2):
        lift_out[v] = lifted[v].astype(BF16)
    epi = product_nt(jnp.concatenate(epi_left, axis=1), jnp.concatenate(epi_right, axis=1))
    spatial = product_nt(
        jnp.concatenate(spatial_left, axis=1), jnp.concatenate(spatial_right, axis=1)
    )
    pieces = (
        spatial[:, :128],
        epi[:, :128],
        jnp.concatenate([spatial[:, 128:], epi[:, 128:]], axis=1),
        jnp.concatenate([up_total, jnp.zeros_like(up_total)], axis=1),
    )
    start = 0
    for piece in pieces:
        end = start + piece.shape[0]
        pay_ref[start:end] = piece
        start = end


def dealt_views(own_ref, one_ref, two_ref, chans):
    before, after = sides("ang", 4)
    return [
        chosen(before, one_ref[1, 2 * chans :], two_ref[1, 2 * chans :]),
        own_ref[0, 2 * chans :],
        own_ref[1, 2 * chans :],
        chosen(after, one_ref[0, 2 * chans :], two_ref[0, 2 * chans :]),
    ]


def main_inner_kernel(
    own_ref, mixed_one_ref, mixed_two_ref, light_ref, out_ref, epi_ref, back_ref, lift_ref, drop_ref, pay_ref, lift_out
):
    def near(v, h):
        return [light_ref[v, h + k] for k in (-1, 0, 1)]

    main_rows(
        (1, 2),
        (own_ref, mixed_one_ref, mixed_two_ref),
        dealt_views(own_ref, mixed_one_ref, mixed_two_ref, light_ref.shape[2]),
        near,
        out_ref,
        epi_ref,
        back_ref,
        lift_ref,
        drop_ref,
        pay_ref,
        lift_out,
    )


def main_edge_kernel(
    first_ref,
    first_one_ref,
    first_two_ref,
    own_ref,
    mixed_one_ref,
    mixed_two_ref,
    light_ref,
    one_ref,
    two_ref,
    out_ref,
    epi_ref,
    back_ref,
    lift_ref,
    drop_ref,
    inner_pay_ref,
    pay_ref,
    lift_out,
):
    above, below = sides(ROWS, 16)

    def near(v, h):
        if h == 0:
            return [chosen(above, one_ref[v, 0], two_ref[v, 0]), light_ref[v, 0], light_ref[v, 1]]
        return [light_ref[v, 2], light_ref[v, 3], chosen(below, one_ref[v, 0], two_ref[v, 0])]

    main_rows(
        (0, 3),
        (first_ref, first_one_ref, first_two_ref),
        dealt_views(own_ref, mixed_one_ref, mixed_two_ref, light_ref.shape[2]),
        near,
        out_ref,
        epi_ref,
        back_ref,
        lift_ref,
        drop_ref,
        pay_ref,
        lift_out,
    )
    pay_ref[...] += inner_pay_ref[...]


def weave_kernel(inner_ref, edge_ref, deal_ref, up_ref):
    size = deal_ref.shape[0]
    lanes = size // 4
    lifted = [inner_ref[v] + edge_ref[v] for v in range(2)]
    for block in range(up_ref.shape[2] // size):
        spread = [
            jnp.concatenate(
                [
                    lifted[v][q * 16 : (q + 1) * 16, block * lanes : (block + 1) * lanes]
                    for q in range(4)
                ],
                axis=1,
            )
            for v in range(2)
        ]
        woven = product_nt(jnp.concatenate(spread, axis=0), deal_ref[...]).astype(BF16)
        for v in range(2):
            up_ref[v, :, block * size : (block + 1) * size] = woven[v * 16 : (v + 1) * 16]


def unpack_kernel(sent_ref, spatial_ref, epi_ref, up_ref, pay_ref):
    pay_ref[...] = sent_ref[...].astype(F32)
    chans = spatial_ref.shape[2]
    three = 3 * chans
    for which, ref in enumerate((spatial_ref, epi_ref)):
        for j in range(3):
            both = pay_ref[which * three + j * chans : which * three + (j + 1) * chans, :]
            ref[0, j] = both[:, :chans]
            ref[1, j] = both[:, chans:]
            last = pay_ref[2 * three + j * chans : 2 * three + (j + 1) * chans, :]
            ref[2, j] = last[:, which * chans : (which + 1) * chans]
    for p in range(4):
        for q in range(4):
            base = 3 * three + q * 16 + p
            total = pay_ref[base : base + 1, :chans]
            for h in range(1, 4):
                total = total + pay_ref[base + 4 * h : base + 4 * h + 1, :chans]
            up_ref[4 * p + q : 4 * p + q + 1, :] = total


def local_call(kernel, shapes, name, *operands, micros=3, loose=(), scratch=()):
    operands = [
        pltpu.with_memory_space_constraint(operand, pltpu.HBM if place in loose else pltpu.VMEM)
        for place, operand in enumerate(operands)
    ]
    return pl.pallas_call(
        kernel,
        out_shape=shapes,
        scratch_shapes=scratch,
        in_specs=[
            pl.BlockSpec(memory_space=pltpu.HBM if place in loose else pltpu.VMEM)
            for place in range(len(operands))
        ],
        cost_estimate=pl.CostEstimate(
            flops=micros * 1_000_000_000, bytes_accessed=micros * 3_000_000, transcendentals=0
        ),
        compiler_params=pltpu.CompilerParams(vmem_limit_bytes=VMEM_LIMIT),
        name=name,
    )(*operands)


def on_device(light_field, spatial_weight, epi_weight, upsample_weight, image_grad):
    _, _, views, rows, chans, breadth = light_field.shape
    light = light_field.reshape(views, rows, chans, breadth)
    image = image_grad.reshape(views, image_grad.shape[3], image_grad.shape[4])

    three = 3 * chans
    like = pltpu.VMEM
    plain = jax.ShapeDtypeStruct
    half_out = like((views, 2, chans, breadth), F32)
    taps = like((three, three), BF16)
    edge_line = like((views, 1, chans, breadth), BF16)
    (
        mixed,
        inner_out,
        deal,
        spatial_taps,
        epi_taps,
        back_taps,
        lift,
        drop,
        light_here,
        send_one,
        send_two,
    ) = local_call(
        inner_kernel,
        (
            like((views, 2 * chans + 64, breadth), BF16),
            half_out,
            like((512, 512), BF16),
            taps,
            taps,
            taps,
            like((rows, 64, chans), BF16),
            like((rows, chans, 64), BF16),
            like(light.shape, BF16),
            edge_line,
            edge_line,
        ),
        "inner",
        image,
        light,
        spatial_weight,
        epi_weight,
        upsample_weight,
        loose=(0, 1, 2, 3, 4),
        scratch=[
            pltpu.VMEM(image.shape, BF16),
            pltpu.VMEM(spatial_weight.shape, BF16),
            pltpu.VMEM(epi_weight.shape, BF16),
            pltpu.VMEM(upsample_weight.shape, BF16),
            pltpu.SemaphoreType.DMA((5,)),
        ],
    )
    light = light_here
    line_one, line_two = with_next_and_before(send_one, send_two, ROWS)
    mixed_one, mixed_two = with_next_and_before(mixed, mixed, "ang")
    first, edge_out = local_call(
        edge_kernel,
        (like((views, 2 * chans, breadth), BF16), half_out),
        "edge",
        light,
        line_one,
        line_two,
        spatial_taps,
    )
    first_one, first_two = with_next_and_before(first, first, "ang")

    weights = (epi_taps, back_taps, lift, drop)
    lift_half = like((views, 64, breadth), BF16)
    whole_pay = like((640, 128), F32)
    inner_pay, inner_lift = local_call(
        main_inner_kernel,
        (whole_pay, lift_half),
        "main_inner",
        mixed,
        mixed_one,
        mixed_two,
        light,
        inner_out,
        *weights,
    )
    pay, edge_lift = local_call(
        main_edge_kernel,
        (whole_pay, lift_half),
        "main_edge",
        first,
        first_one,
        first_two,
        mixed,
        mixed_one,
        mixed_two,
        light,
        line_one,
        line_two,
        edge_out,
        *weights,
        inner_pay,
    )
    up = local_call(
        weave_kernel, plain(image.shape, BF16), "weave", inner_lift, edge_lift, deal
    )
    spatial_grad, epi_grad, up_grad = local_call(
        unpack_kernel,
        (
            plain(spatial_weight.shape, F32),
            plain(epi_weight.shape, F32),
            plain(upsample_weight.shape, F32),
        ),
        "unpack",
        sum_everywhere(pay),
        scratch=[pltpu.VMEM((640, 128), F32)],
    )
    return (up.reshape(image_grad.shape), spatial_grad, epi_grad, up_grad)


def solution(mesh):
    split = Mesh(mesh.devices.reshape(2, 2, 4, 4, 4), ("pair", "core", "ang", "quad", "x"))
    image_spec = P(DP, None, "ang", ROWS, None)
    return jax.shard_map(
        on_device,
        mesh=split,
        in_specs=(P(DP, None, "ang", ROWS, None, None), P(), P(), P(), image_spec),
        out_specs=(image_spec, P(), P(), P()),
        check_vma=False,
    )
```

```python
import jax
import jax.numpy as jnp
from jax import lax
from jax.experimental import pallas as pl
from jax.experimental.pallas import tpu as pltpu
from jax.sharding import Mesh
from jax.sharding import PartitionSpec as P

F32 = jnp.float32
BF16 = jnp.bfloat16
DP = ("pair", "core")
ROWS = ("quad", "x")
VMEM_LIMIT = 40 * 1024 * 1024


def swapped(value, axis, step):
    count = lax.axis_size(axis)
    return lax.ppermute(value, axis, [(i, (i + step) % count) for i in range(count)])


def sum_everywhere(pay):
    plane = ("ang", "x")
    rows = pay.shape[0]
    mine = lax.all_to_all(
        pay.reshape(16, rows // 16, 128), plane, split_axis=0, concat_axis=0, tiled=True
    ).sum(0)
    mine = mine + swapped(mine, "core", 1)
    for flip in (1, 3):
        mine = mine + lax.ppermute(mine, "quad", [(i, i ^ flip) for i in range(4)])
    spread = jnp.broadcast_to(mine.astype(BF16)[None], (32,) + mine.shape)
    gathered = lax.all_to_all(spread, ("pair",) + plane, split_axis=0, concat_axis=0, tiled=True)
    return gathered.reshape(2, rows, 128)


def is_even(axis):
    return lax.axis_index(axis) % 2 == 0


def with_next_and_before(first_send, second_send, axis):
    count = lax.axis_size(axis)
    axes = (axis,) if isinstance(axis, str) else axis
    pairs = [(count - 1, 2 * count - 1), (0, count)]
    for core in (0, count):
        pairs += [(core + i, core + i + 1) for i in range(1, count - 1, 2)]
    two = lax.ppermute(second_send, ("core",) + axes, pairs + [(j, i) for i, j in pairs])
    one = lax.ppermute(first_send, axis, [(i, i ^ 1) for i in range(count)])
    return one, two


def has_neighbours(axis, count):
    place = lax.axis_index(axis)
    return place > 0, place < count - 1


def chosen(flags, one, two):
    even, present = flags
    values = jnp.where(even, one, two)
    return jnp.where(present, values, jnp.zeros_like(values))


def sides(axis, count):
    even = is_even(axis)
    before, after = has_neighbours(axis, count)
    return (jnp.logical_not(even), before), (even, after)


def column(shape):
    return lax.broadcasted_iota(jnp.int32, shape, len(shape) - 1)


def from_left(values):
    return jnp.where(column(values.shape) == 0, 0.0, pltpu.roll(values, 1, axis=1))


def from_right(values):
    width = values.shape[1]
    return jnp.where(column(values.shape) == width - 1, 0.0, pltpu.roll(values, width - 1, axis=1))


def product(left, right):
    return jnp.dot(left, right, preferred_element_type=F32)


def product_nt(left, right):
    return lax.dot_general(left, right, (((1,), (1,)), ((), ())), preferred_element_type=F32)


def gate_of(values):
    return 0.5 * jnp.tanh(0.5 * values) + 0.5


def silu_slope(values, gate):
    return gate * (1.0 + values * (1.0 - gate))


def taps_of(slope):
    return jnp.concatenate(
        [from_right(slope).astype(BF16), slope.astype(BF16), from_left(slope).astype(BF16)], axis=0
    )


def conv_taps(weights, stacked, forward):
    taps = product(weights, stacked)
    chans = weights.shape[0] // 3
    left, right = (from_left, from_right) if forward else (from_right, from_left)
    return taps[chans : 2 * chans] + left(taps[:chans]) + right(taps[2 * chans :])


def unit(size):
    return jnp.where(
        lax.broadcasted_iota(jnp.int32, (size, size), 0)
        == lax.broadcasted_iota(jnp.int32, (size, size), 1),
        1.0,
        0.0,
    ).astype(BF16)


def forward_taps(ref, taps_ref):
    chans = ref.shape[2]
    for j in range(3):
        taps_ref[j * chans : (j + 1) * chans] = jnp.concatenate([ref[i, j] for i in range(3)], axis=1)


def prepare_weights(spatial_ref, epi_ref, up_ref, taps_ref, epi_taps_ref, back_ref, lift_ref, drop_ref):
    chans = spatial_ref.shape[2]
    forward_taps(spatial_ref, taps_ref)
    forward_taps(epi_ref, epi_taps_ref)
    stacked = jnp.concatenate(
        [jnp.concatenate([epi_ref[2 - s, j] for j in range(3)], axis=1) for s in range(3)], axis=0
    )
    back_ref[...] = product_nt(unit(3 * chans), stacked).astype(BF16)
    turned = product_nt(unit(chans), up_ref[...]).astype(BF16)
    line = lax.broadcasted_iota(jnp.int32, (64, 16), 0)
    sub = lax.broadcasted_iota(jnp.int32, (64, 16), 1)
    match = sub == 4 * (line % 4) + line // 16
    for h in range(4):
        pick = jnp.where(match & ((line % 16) // 4 == h), 1.0, 0.0).astype(BF16)
        lift_ref[h] = product(pick, up_ref[...]).astype(BF16)
        drop_ref[h] = product_nt(turned, pick).astype(BF16)


def inner_kernel(
    image_hbm,
    light_hbm,
    spatial_hbm,
    epi_hbm,
    up_hbm,
    mixed_one_ref,
    mixed_two_ref,
    dealt_ref,
    out_ref,
    deal_ref,
    weight_ref,
    epi_taps_ref,
    back_ref,
    lift_ref,
    drop_ref,
    light_ref,
    one_ref,
    two_ref,
    image_ref,
    spatial_ref,
    epi_ref,
    up_ref,
    sems,
):
    pairs = (
        (spatial_hbm, spatial_ref),
        (image_hbm, image_ref),
        (light_hbm, light_ref),
        (epi_hbm, epi_ref),
        (up_hbm, up_ref),
    )
    copies = [
        pltpu.make_async_copy(source, target, sems.at[place])
        for place, (source, target) in enumerate(pairs)
    ]
    for copy in copies:
        copy.start()
    size = deal_ref.shape[0]
    source = lax.broadcasted_iota(jnp.int32, (size, size), 0)
    target = lax.broadcasted_iota(jnp.int32, (size, size), 1)
    lanes = size // 4
    wanted = 4 * (target % lanes) + target // lanes
    deal = jnp.where(source == wanted, 1.0, 0.0).astype(BF16)
    deal_ref[...] = deal
    chans = light_ref.shape[2]
    for copy in copies:
        copy.wait()
    even = is_even(ROWS)
    last = light_ref.shape[1] - 1
    for view in range(2):
        one_ref[view, 0] = jnp.where(even, light_ref[view, last], light_ref[view, 0])
        two_ref[view, 0] = jnp.where(even, light_ref[view, 0], light_ref[view, last])
    prepare_weights(
        spatial_ref, epi_ref, up_ref, weight_ref, epi_taps_ref, back_ref, lift_ref, drop_ref
    )
    for block in range(image_ref.shape[2] // size):
        cut = slice(block * size, (block + 1) * size)
        stacked = jnp.concatenate([image_ref[0, :, cut], image_ref[1, :, cut]], axis=0)
        moved = product(stacked, deal).astype(BF16)
        for view in range(2):
            for q in range(4):
                dealt_ref[
                    view, q * 16 : (q + 1) * 16, block * lanes : (block + 1) * lanes
                ] = moved[view * 16 : (view + 1) * 16, q * lanes : (q + 1) * lanes]
    even_view = is_even("ang")
    mixed_one_ref[4 * chans :] = jnp.where(even_view, dealt_ref[1], dealt_ref[0])
    mixed_two_ref[4 * chans :] = jnp.where(even_view, dealt_ref[0], dealt_ref[1])
    for view in range(2):
        for slot, h in enumerate((1, 2)):
            stacked = jnp.concatenate([light_ref[view, h + k] for k in (-1, 0, 1)], axis=0)
            total = conv_taps(weight_ref[...], stacked, True)
            gate = gate_of(total)
            out_ref[view, slot] = silu_slope(total, gate)
            first = (light_ref[view, h].astype(F32) + total * gate).astype(BF16)
            cut = slice((2 * view + slot) * chans, (2 * view + slot + 1) * chans)
            mixed_one_ref[cut] = first
            mixed_two_ref[cut] = first


def edge_kernel(light_ref, one_ref, two_ref, weight_ref, first_ref, out_ref):
    chans = light_ref.shape[2]
    above, below = sides(ROWS, 16)
    for view in range(2):
        for slot, h in enumerate((0, 3)):
            if slot == 0:
                stacked = [chosen(above, one_ref[view, 0], two_ref[view, 0]), light_ref[view, 0], light_ref[view, 1]]
            else:
                stacked = [light_ref[view, 2], light_ref[view, 3], chosen(below, one_ref[view, 0], two_ref[view, 0])]
            total = conv_taps(weight_ref[...], jnp.concatenate(stacked, axis=0), True)
            gate = gate_of(total)
            out_ref[view, slot] = silu_slope(total, gate)
            first = light_ref[view, h].astype(F32) + total * gate
            cut = slice((2 * view + slot) * chans, (2 * view + slot + 1) * chans)
            first_ref[cut] = first.astype(BF16)


def main_rows(rows, firsts, dealt, grad_of, near, out_ref, epi_ref, back_ref, lift_ref, pay_ref, lift_out):
    chans = out_ref.shape[2]
    three = 3 * chans
    lifted = [None, None]
    up_total = None
    epi_left, epi_right, spatial_left, spatial_right = [], [], [], []
    before, after = sides("ang", 4)
    for slot, h in enumerate(rows):
        cuts = [slice((2 * v + slot) * chans, (2 * v + slot + 1) * chans) for v in range(2)]
        stack = jnp.concatenate(
            [chosen(before, firsts[1][cut], firsts[2][cut]) for cut in cuts]
            + [firsts[0][cut] for cut in cuts]
            + [chosen(after, firsts[1][cut], firsts[2][cut]) for cut in cuts],
            axis=0,
        )
        here = (lax.broadcasted_iota(jnp.int32, (64, chans), 0) % 16) // 4 == h
        grads, slopes = [], []
        for v in range(4):
            window = stack[v * chans : (v + 3) * chans]
            total = conv_taps(epi_ref[...], window, True)
            gate = gate_of(total)
            grad = grad_of(slot, v).astype(F32)
            slope = grad * silu_slope(total, gate)
            slopes.append(slope.astype(BF16))
            if v in (1, 2):
                grads.append(grad)
                own = stack[(v + 1) * chans : (v + 2) * chans]
                second = (own.astype(F32) + total * gate).astype(BF16)
                part = product(lift_ref[h], second)
                lifted[v - 1] = part if slot == 0 else lifted[v - 1] + part
                part = jnp.where(here, product_nt(dealt[v], second), 0.0)
                up_total = part if up_total is None else up_total + part
                epi_left.append(taps_of(slope))
                epi_right.append(window)
        slopes = jnp.concatenate(slopes, axis=0)
        for v in range(2):
            moved = conv_taps(back_ref[...], slopes[v * chans : (v + 3) * chans], False)
            first_grad = (grads[v] + moved).astype(BF16).astype(F32)
            slope = first_grad * out_ref[v, slot]
            spatial_left.append(taps_of(slope))
            spatial_right.append(jnp.concatenate(near(v, h), axis=0))
    for v in range(2):
        lift_out[v] = lifted[v].astype(BF16)
    epi = product_nt(jnp.concatenate(epi_left, axis=1), jnp.concatenate(epi_right, axis=1))
    spatial = product_nt(
        jnp.concatenate(spatial_left, axis=1), jnp.concatenate(spatial_right, axis=1)
    )
    pieces = (
        spatial[:, :128],
        epi[:, :128],
        jnp.concatenate([spatial[:, 128:], epi[:, 128:]], axis=1),
        jnp.concatenate([up_total, jnp.zeros_like(up_total)], axis=1),
    )
    start = 0
    for piece in pieces:
        end = start + piece.shape[0]
        pay_ref[start:end] = piece
        start = end


def dealt_views(dealt_ref, one_ref, two_ref, chans):
    before, after = sides("ang", 4)
    one, two = one_ref[4 * chans :], two_ref[4 * chans :]
    return [chosen(before, one, two), dealt_ref[0], dealt_ref[1], chosen(after, one, two)]


def main_inner_kernel(
    own_ref,
    mixed_one_ref,
    mixed_two_ref,
    dealt_ref,
    light_ref,
    out_ref,
    epi_ref,
    back_ref,
    lift_ref,
    drop_ref,
    pay_ref,
    lift_out,
    edge_grad_ref,
):
    dealt = dealt_views(dealt_ref, mixed_one_ref, mixed_two_ref, light_ref.shape[2])
    for slot, h in enumerate((0, 3)):
        for v in range(4):
            edge_grad_ref[slot, v] = product(drop_ref[h], dealt[v]).astype(BF16)

    def grad_of(slot, v):
        return product(drop_ref[slot + 1], dealt[v]).astype(BF16)

    def near(v, h):
        return [light_ref[v, h + k] for k in (-1, 0, 1)]

    main_rows(
        (1, 2),
        (own_ref, mixed_one_ref, mixed_two_ref),
        dealt,
        grad_of,
        near,
        out_ref,
        epi_ref,
        back_ref,
        lift_ref,
        pay_ref,
        lift_out,
    )


def main_edge_kernel(
    first_ref,
    first_one_ref,
    first_two_ref,
    dealt_ref,
    edge_grad_ref,
    light_ref,
    one_ref,
    two_ref,
    out_ref,
    epi_ref,
    back_ref,
    lift_ref,
    inner_pay_ref,
    pay_ref,
    lift_out,
):
    above, below = sides(ROWS, 16)

    def near(v, h):
        if h == 0:
            return [chosen(above, one_ref[v, 0], two_ref[v, 0]), light_ref[v, 0], light_ref[v, 1]]
        return [light_ref[v, 2], light_ref[v, 3], chosen(below, one_ref[v, 0], two_ref[v, 0])]

    main_rows(
        (0, 3),
        (first_ref, first_one_ref, first_two_ref),
        (None, dealt_ref[0], dealt_ref[1], None),
        lambda slot, v: edge_grad_ref[slot, v],
        near,
        out_ref,
        epi_ref,
        back_ref,
        lift_ref,
        pay_ref,
        lift_out,
    )
    pay_ref[...] += inner_pay_ref[...]


def weave_kernel(inner_ref, edge_ref, deal_ref, up_ref):
    size = deal_ref.shape[0]
    lanes = size // 4
    lifted = [inner_ref[v] + edge_ref[v] for v in range(2)]
    for block in range(up_ref.shape[2] // size):
        spread = [
            jnp.concatenate(
                [
                    lifted[v][q * 16 : (q + 1) * 16, block * lanes : (block + 1) * lanes]
                    for q in range(4)
                ],
                axis=1,
            )
            for v in range(2)
        ]
        woven = product_nt(jnp.concatenate(spread, axis=0), deal_ref[...]).astype(BF16)
        for v in range(2):
            up_ref[v, :, block * size : (block + 1) * size] = woven[v * 16 : (v + 1) * 16]


def unpack_kernel(sent_ref, spatial_ref, epi_ref, up_ref, pay_ref):
    pay_ref[...] = sent_ref[0].astype(F32) + sent_ref[1].astype(F32)
    chans = spatial_ref.shape[2]
    three = 3 * chans
    for which, ref in enumerate((spatial_ref, epi_ref)):
        for j in range(3):
            both = pay_ref[which * three + j * chans : which * three + (j + 1) * chans, :]
            ref[0, j] = both[:, :chans]
            ref[1, j] = both[:, chans:]
            last = pay_ref[2 * three + j * chans : 2 * three + (j + 1) * chans, :]
            ref[2, j] = last[:, which * chans : (which + 1) * chans]
    for p in range(4):
        for q in range(4):
            base = 3 * three + q * 16 + p
            total = pay_ref[base : base + 1, :chans]
            for h in range(1, 4):
                total = total + pay_ref[base + 4 * h : base + 4 * h + 1, :chans]
            up_ref[4 * p + q : 4 * p + q + 1, :] = total


def local_call(kernel, shapes, name, *operands, micros=3, loose=(), scratch=()):
    operands = [
        pltpu.with_memory_space_constraint(operand, pltpu.HBM if place in loose else pltpu.VMEM)
        for place, operand in enumerate(operands)
    ]
    return pl.pallas_call(
        kernel,
        out_shape=shapes,
        scratch_shapes=scratch,
        in_specs=[
            pl.BlockSpec(memory_space=pltpu.HBM if place in loose else pltpu.VMEM)
            for place in range(len(operands))
        ],
        cost_estimate=pl.CostEstimate(
            flops=micros * 1_000_000_000, bytes_accessed=micros * 3_000_000, transcendentals=0
        ),
        compiler_params=pltpu.CompilerParams(vmem_limit_bytes=VMEM_LIMIT),
        name=name,
    )(*operands)


def on_device(light_field, spatial_weight, epi_weight, upsample_weight, image_grad):
    _, _, views, rows, chans, breadth = light_field.shape
    light = light_field.reshape(views, rows, chans, breadth)
    image = image_grad.reshape(views, image_grad.shape[3], image_grad.shape[4])

    three = 3 * chans
    like = pltpu.VMEM
    plain = jax.ShapeDtypeStruct
    half_out = like((views, 2, chans, breadth), F32)
    taps = like((three, three), BF16)
    edge_line = like((views, 1, chans, breadth), BF16)
    (
        mixed_for_one,
        mixed_for_two,
        dealt,
        inner_out,
        deal,
        spatial_taps,
        epi_taps,
        back_taps,
        lift,
        drop,
        light_here,
        send_one,
        send_two,
    ) = local_call(
        inner_kernel,
        (
            like((4 * chans + 64, breadth), BF16),
            like((4 * chans + 64, breadth), BF16),
            like((views, 64, breadth), BF16),
            half_out,
            like((512, 512), BF16),
            taps,
            taps,
            taps,
            like((rows, 64, chans), BF16),
            like((rows, chans, 64), BF16),
            like(light.shape, BF16),
            edge_line,
            edge_line,
        ),
        "inner",
        image,
        light,
        spatial_weight,
        epi_weight,
        upsample_weight,
        loose=(0, 1, 2, 3, 4),
        scratch=[
            pltpu.VMEM(image.shape, BF16),
            pltpu.VMEM(spatial_weight.shape, BF16),
            pltpu.VMEM(epi_weight.shape, BF16),
            pltpu.VMEM(upsample_weight.shape, BF16),
            pltpu.SemaphoreType.DMA((5,)),
        ],
    )
    light = light_here
    line_one, line_two = with_next_and_before(send_one, send_two, ROWS)
    mixed_one, mixed_two = with_next_and_before(mixed_for_one, mixed_for_two, "ang")
    first, edge_out = local_call(
        edge_kernel,
        (like((4 * chans, breadth), BF16), half_out),
        "edge",
        light,
        line_one,
        line_two,
        spatial_taps,
    )
    first_one, first_two = with_next_and_before(first, first, "ang")

    lift_half = like((views, 64, breadth), BF16)
    whole_pay = like((640, 128), F32)
    inner_pay, inner_lift, edge_grad = local_call(
        main_inner_kernel,
        (whole_pay, lift_half, like((2, 4, chans, breadth), BF16)),
        "main_inner",
        mixed_for_one,
        mixed_one,
        mixed_two,
        dealt,
        light,
        inner_out,
        epi_taps,
        back_taps,
        lift,
        drop,
    )
    pay, edge_lift = local_call(
        main_edge_kernel,
        (whole_pay, lift_half),
        "main_edge",
        first,
        first_one,
        first_two,
        dealt,
        edge_grad,
        light,
        line_one,
        line_two,
        edge_out,
        epi_taps,
        back_taps,
        lift,
        inner_pay,
    )
    up = local_call(
        weave_kernel, plain(image.shape, BF16), "weave", inner_lift, edge_lift, deal
    )
    spatial_grad, epi_grad, up_grad = local_call(
        unpack_kernel,
        (
            plain(spatial_weight.shape, F32),
            plain(epi_weight.shape, F32),
            plain(upsample_weight.shape, F32),
        ),
        "unpack",
        sum_everywhere(pay),
        scratch=[pltpu.VMEM((640, 128), F32)],
    )
    return (up.reshape(image_grad.shape), spatial_grad, epi_grad, up_grad)


def solution(mesh):
    split = Mesh(mesh.devices.reshape(2, 2, 4, 4, 4), ("pair", "core", "ang", "quad", "x"))
    image_spec = P(DP, None, "ang", ROWS, None)
    return jax.shard_map(
        on_device,
        mesh=split,
        in_specs=(P(DP, None, "ang", ROWS, None, None), P(), P(), P(), image_spec),
        out_specs=(image_spec, P(), P(), P()),
        check_vma=False,
    )
```

```python
import jax
import jax.numpy as jnp
from jax import lax
from jax.experimental import pallas as pl
from jax.experimental.pallas import tpu as pltpu
from jax.sharding import Mesh
from jax.sharding import PartitionSpec as P

F32 = jnp.float32
BF16 = jnp.bfloat16
DP = ("pair", "core")
ROWS = ("quad", "x")
VMEM_LIMIT = 40 * 1024 * 1024


def swapped(value, axis, step):
    count = lax.axis_size(axis)
    return lax.ppermute(value, axis, [(i, (i + step) % count) for i in range(count)])


def sum_everywhere(pay):
    plane = ("ang", "x")
    rows = pay.shape[0]
    mine = lax.all_to_all(
        pay.reshape(16, rows // 16, 128), plane, split_axis=0, concat_axis=0, tiled=True
    ).sum(0)
    mine = mine + swapped(mine, "core", 1)
    for flip in (1, 3):
        mine = mine + lax.ppermute(mine, "quad", [(i, i ^ flip) for i in range(4)])
    spread = jnp.broadcast_to(mine.astype(BF16)[None], (32,) + mine.shape)
    gathered = lax.all_to_all(spread, ("pair",) + plane, split_axis=0, concat_axis=0, tiled=True)
    return gathered.reshape(2, rows, 128)


def is_even(axis):
    return lax.axis_index(axis) % 2 == 0


def with_next_and_before(first_send, second_send, axis):
    count = lax.axis_size(axis)
    axes = (axis,) if isinstance(axis, str) else axis
    pairs = [(count - 1, 2 * count - 1), (0, count)]
    for core in (0, count):
        pairs += [(core + i, core + i + 1) for i in range(1, count - 1, 2)]
    two = lax.ppermute(second_send, ("core",) + axes, pairs + [(j, i) for i, j in pairs])
    one = lax.ppermute(first_send, axis, [(i, i ^ 1) for i in range(count)])
    return one, two


def has_neighbours(axis, count):
    place = lax.axis_index(axis)
    return place > 0, place < count - 1


def chosen(flags, one, two):
    even, present = flags
    values = jnp.where(even, one, two)
    return jnp.where(present, values, jnp.zeros_like(values))


def sides(axis, count):
    even = is_even(axis)
    before, after = has_neighbours(axis, count)
    return (jnp.logical_not(even), before), (even, after)


def column(shape):
    return lax.broadcasted_iota(jnp.int32, shape, len(shape) - 1)


def from_left(values):
    rolled = pltpu.roll(values, 1, axis=1)
    return jnp.where(column(values.shape) == 0, jnp.zeros_like(rolled), rolled)


def from_right(values):
    width = values.shape[1]
    rolled = pltpu.roll(values, width - 1, axis=1)
    return jnp.where(column(values.shape) == width - 1, jnp.zeros_like(rolled), rolled)


def product(left, right):
    return jnp.dot(left, right, preferred_element_type=F32)


def product_nt(left, right):
    return lax.dot_general(left, right, (((1,), (1,)), ((), ())), preferred_element_type=F32)


def gate_of(values):
    return 0.5 * jnp.tanh(0.5 * values) + 0.5


def silu_slope(values, gate):
    return gate * (1.0 + values * (1.0 - gate))


def taps_of(slope):
    slope = slope.astype(BF16)
    return jnp.concatenate([from_right(slope), slope, from_left(slope)], axis=0)


def conv_taps(weights, stacked, forward):
    return join_taps(product(weights, stacked), forward)


def join_taps(taps, forward):
    chans = taps.shape[0] // 3
    left, right = (from_left, from_right) if forward else (from_right, from_left)
    return taps[chans : 2 * chans] + left(taps[:chans]) + right(taps[2 * chans :])


def unit(size):
    return jnp.where(
        lax.broadcasted_iota(jnp.int32, (size, size), 0)
        == lax.broadcasted_iota(jnp.int32, (size, size), 1),
        1.0,
        0.0,
    ).astype(BF16)


def forward_taps(ref, taps_ref):
    chans = ref.shape[2]
    for j in range(3):
        taps_ref[j * chans : (j + 1) * chans] = jnp.concatenate([ref[i, j] for i in range(3)], axis=1)


def prepare_weights(spatial_ref, epi_ref, up_ref, taps_ref, epi_taps_ref, back_ref, drop_ref):
    chans = spatial_ref.shape[2]
    forward_taps(spatial_ref, taps_ref)
    forward_taps(epi_ref, epi_taps_ref)
    stacked = jnp.concatenate(
        [jnp.concatenate([epi_ref[2 - s, j] for j in range(3)], axis=1) for s in range(3)], axis=0
    )
    back = product_nt(unit(3 * chans), stacked).astype(BF16)
    turned = product_nt(unit(chans), up_ref[...]).astype(BF16)
    line = lax.broadcasted_iota(jnp.int32, (64, 16), 0)
    sub = lax.broadcasted_iota(jnp.int32, (64, 16), 1)
    match = sub == 4 * (line % 4) + line // 16
    for h in range(4):
        pick = jnp.where(match & ((line % 16) // 4 == h), 1.0, 0.0).astype(BF16)
        lift = product(pick, up_ref[...]).astype(BF16)
        back_ref[h, : 3 * chans] = jnp.concatenate([back, jnp.zeros((3 * chans, 64), BF16)], axis=1)
        back_ref[h, 3 * chans :] = jnp.concatenate(
            [jnp.zeros((64, 3 * chans), BF16), lift], axis=1
        )
        drop_ref[h] = product_nt(turned, pick).astype(BF16)


def inner_kernel(
    image_hbm,
    light_hbm,
    spatial_hbm,
    epi_hbm,
    up_hbm,
    mixed_one_ref,
    mixed_two_ref,
    dealt_ref,
    out_ref,
    deal_ref,
    weight_ref,
    epi_taps_ref,
    back_ref,
    drop_ref,
    light_ref,
    one_ref,
    two_ref,
    image_ref,
    spatial_ref,
    epi_ref,
    up_ref,
    sems,
):
    pairs = (
        (spatial_hbm, spatial_ref),
        (image_hbm, image_ref),
        (light_hbm, light_ref),
        (epi_hbm, epi_ref),
        (up_hbm, up_ref),
    )
    copies = [
        pltpu.make_async_copy(source, target, sems.at[place])
        for place, (source, target) in enumerate(pairs)
    ]
    for copy in copies:
        copy.start()
    size = deal_ref.shape[0]
    source = lax.broadcasted_iota(jnp.int32, (size, size), 0)
    target = lax.broadcasted_iota(jnp.int32, (size, size), 1)
    lanes = size // 4
    wanted = 4 * (target % lanes) + target // lanes
    deal = jnp.where(source == wanted, 1.0, 0.0).astype(BF16)
    deal_ref[...] = deal
    chans = light_ref.shape[2]
    for copy in copies:
        copy.wait()
    even = is_even(ROWS)
    last = light_ref.shape[1] - 1
    for view in range(2):
        one_ref[view, 0] = jnp.where(even, light_ref[view, last], light_ref[view, 0])
        two_ref[view, 0] = jnp.where(even, light_ref[view, 0], light_ref[view, last])
    prepare_weights(
        spatial_ref, epi_ref, up_ref, weight_ref, epi_taps_ref, back_ref, drop_ref
    )
    for block in range(image_ref.shape[2] // size):
        cut = slice(block * size, (block + 1) * size)
        stacked = jnp.concatenate([image_ref[0, :, cut], image_ref[1, :, cut]], axis=0)
        moved = product(stacked, deal).astype(BF16)
        for view in range(2):
            for q in range(4):
                dealt_ref[
                    view, q * 16 : (q + 1) * 16, block * lanes : (block + 1) * lanes
                ] = moved[view * 16 : (view + 1) * 16, q * lanes : (q + 1) * lanes]
    even_view = is_even("ang")
    mixed_one_ref[4 * chans :] = jnp.where(even_view, dealt_ref[1], dealt_ref[0])
    mixed_two_ref[4 * chans :] = jnp.where(even_view, dealt_ref[0], dealt_ref[1])
    for view in range(2):
        for slot, h in enumerate((1, 2)):
            stacked = jnp.concatenate([light_ref[view, h + k] for k in (-1, 0, 1)], axis=0)
            total = conv_taps(weight_ref[...], stacked, True)
            gate = gate_of(total)
            out_ref[view, slot] = silu_slope(total, gate)
            first = (light_ref[view, h].astype(F32) + total * gate).astype(BF16)
            cut = slice((2 * view + slot) * chans, (2 * view + slot + 1) * chans)
            mixed_one_ref[cut] = first
            mixed_two_ref[cut] = first


def edge_kernel(light_ref, one_ref, two_ref, weight_ref, first_ref, out_ref):
    chans = light_ref.shape[2]
    above, below = sides(ROWS, 16)
    for view in range(2):
        for slot, h in enumerate((0, 3)):
            if slot == 0:
                stacked = [chosen(above, one_ref[view, 0], two_ref[view, 0]), light_ref[view, 0], light_ref[view, 1]]
            else:
                stacked = [light_ref[view, 2], light_ref[view, 3], chosen(below, one_ref[view, 0], two_ref[view, 0])]
            total = conv_taps(weight_ref[...], jnp.concatenate(stacked, axis=0), True)
            gate = gate_of(total)
            out_ref[view, slot] = silu_slope(total, gate)
            first = light_ref[view, h].astype(F32) + total * gate
            cut = slice((2 * view + slot) * chans, (2 * view + slot + 1) * chans)
            first_ref[cut] = first.astype(BF16)


def main_rows(rows, firsts, dealt, grad_of, near, out_ref, epi_ref, back_ref, pay_ref, lift_out):
    chans = out_ref.shape[2]
    three = 3 * chans
    lifted = [None, None]
    epi_left, epi_right, spatial_left, spatial_right = [], [], [], []
    before, after = sides("ang", 4)
    for slot, h in enumerate(rows):
        cuts = [slice((2 * v + slot) * chans, (2 * v + slot + 1) * chans) for v in range(2)]
        stack = jnp.concatenate(
            [chosen(before, firsts[1][cut], firsts[2][cut]) for cut in cuts]
            + [firsts[0][cut] for cut in cuts]
            + [chosen(after, firsts[1][cut], firsts[2][cut]) for cut in cuts],
            axis=0,
        )
        here = (lax.broadcasted_iota(jnp.int32, dealt[1].shape, 0) % 16) // 4 == h
        grads, slopes, seconds = [], [], []
        for v in range(4):
            window = stack[v * chans : (v + 3) * chans]
            total = conv_taps(epi_ref[...], window, True)
            gate = gate_of(total)
            grad = grad_of(slot, v).astype(F32)
            slope = grad * silu_slope(total, gate)
            slopes.append(slope.astype(BF16))
            if v in (1, 2):
                grads.append(grad)
                own = stack[(v + 1) * chans : (v + 2) * chans]
                second = (own.astype(F32) + total * gate).astype(BF16)
                seconds.append(second)
                shown = jnp.where(here, dealt[v], jnp.zeros_like(dealt[v]))
                epi_left.append(jnp.concatenate([taps_of(slope), shown], axis=0))
                epi_right.append(jnp.concatenate([window, second], axis=0))
        slopes = jnp.concatenate(slopes, axis=0)
        for v in range(2):
            below = jnp.concatenate([slopes[v * chans : (v + 3) * chans], seconds[v]], axis=0)
            both = product(back_ref[h], below)
            part = both[three:]
            lifted[v] = part if slot == 0 else lifted[v] + part
            first_grad = (grads[v] + join_taps(both[:three], False)).astype(BF16).astype(F32)
            slope = first_grad * out_ref[v, slot]
            spatial_left.append(taps_of(slope))
            spatial_right.append(jnp.concatenate(near(v, h), axis=0))
    for v in range(2):
        lift_out[v] = lifted[v].astype(BF16)
    epi = product_nt(jnp.concatenate(epi_left, axis=1), jnp.concatenate(epi_right, axis=1))
    spatial = product_nt(
        jnp.concatenate(spatial_left, axis=1), jnp.concatenate(spatial_right, axis=1)
    )
    pieces = (
        spatial[:, :128],
        epi[:three, :128],
        jnp.concatenate([spatial[:, 128:], epi[:three, 128:three]], axis=1),
        jnp.concatenate([epi[three:, three:], jnp.zeros((64, 128 - chans), F32)], axis=1),
    )
    start = 0
    for piece in pieces:
        end = start + piece.shape[0]
        pay_ref[start:end] = piece
        start = end


def dealt_views(dealt_ref, one_ref, two_ref, chans):
    before, after = sides("ang", 4)
    one, two = one_ref[4 * chans :], two_ref[4 * chans :]
    return [chosen(before, one, two), dealt_ref[0], dealt_ref[1], chosen(after, one, two)]


def main_inner_kernel(
    own_ref,
    mixed_one_ref,
    mixed_two_ref,
    dealt_ref,
    light_ref,
    out_ref,
    epi_ref,
    back_ref,
    drop_ref,
    pay_ref,
    lift_out,
    edge_grad_ref,
):
    dealt = dealt_views(dealt_ref, mixed_one_ref, mixed_two_ref, light_ref.shape[2])
    for slot, h in enumerate((0, 3)):
        for v in range(4):
            edge_grad_ref[slot, v] = product(drop_ref[h], dealt[v]).astype(BF16)

    def grad_of(slot, v):
        return product(drop_ref[slot + 1], dealt[v]).astype(BF16)

    def near(v, h):
        return [light_ref[v, h + k] for k in (-1, 0, 1)]

    main_rows(
        (1, 2),
        (own_ref, mixed_one_ref, mixed_two_ref),
        dealt,
        grad_of,
        near,
        out_ref,
        epi_ref,
        back_ref,
        pay_ref,
        lift_out,
    )


def main_edge_kernel(
    first_ref,
    first_one_ref,
    first_two_ref,
    dealt_ref,
    edge_grad_ref,
    light_ref,
    one_ref,
    two_ref,
    out_ref,
    epi_ref,
    back_ref,
    inner_pay_ref,
    pay_ref,
    lift_out,
):
    above, below = sides(ROWS, 16)

    def near(v, h):
        if h == 0:
            return [chosen(above, one_ref[v, 0], two_ref[v, 0]), light_ref[v, 0], light_ref[v, 1]]
        return [light_ref[v, 2], light_ref[v, 3], chosen(below, one_ref[v, 0], two_ref[v, 0])]

    main_rows(
        (0, 3),
        (first_ref, first_one_ref, first_two_ref),
        (None, dealt_ref[0], dealt_ref[1], None),
        lambda slot, v: edge_grad_ref[slot, v],
        near,
        out_ref,
        epi_ref,
        back_ref,
        pay_ref,
        lift_out,
    )
    pay_ref[...] += inner_pay_ref[...]


def weave_kernel(inner_ref, edge_ref, deal_ref, up_ref):
    size = deal_ref.shape[0]
    lanes = size // 4
    lifted = [inner_ref[v] + edge_ref[v] for v in range(2)]
    for block in range(up_ref.shape[2] // size):
        spread = [
            jnp.concatenate(
                [
                    lifted[v][q * 16 : (q + 1) * 16, block * lanes : (block + 1) * lanes]
                    for q in range(4)
                ],
                axis=1,
            )
            for v in range(2)
        ]
        woven = product_nt(jnp.concatenate(spread, axis=0), deal_ref[...]).astype(BF16)
        for v in range(2):
            up_ref[v, :, block * size : (block + 1) * size] = woven[v * 16 : (v + 1) * 16]


def unpack_kernel(sent_ref, spatial_ref, epi_ref, up_ref, pay_ref):
    pay_ref[...] = sent_ref[0].astype(F32) + sent_ref[1].astype(F32)
    chans = spatial_ref.shape[2]
    three = 3 * chans
    for which, ref in enumerate((spatial_ref, epi_ref)):
        for j in range(3):
            both = pay_ref[which * three + j * chans : which * three + (j + 1) * chans, :]
            ref[0, j] = both[:, :chans]
            ref[1, j] = both[:, chans:]
            last = pay_ref[2 * three + j * chans : 2 * three + (j + 1) * chans, :]
            ref[2, j] = last[:, which * chans : (which + 1) * chans]
    for p in range(4):
        for q in range(4):
            base = 3 * three + q * 16 + p
            total = pay_ref[base : base + 1, :chans]
            for h in range(1, 4):
                total = total + pay_ref[base + 4 * h : base + 4 * h + 1, :chans]
            up_ref[4 * p + q : 4 * p + q + 1, :] = total


def local_call(kernel, shapes, name, *operands, micros=3, loose=(), scratch=()):
    operands = [
        pltpu.with_memory_space_constraint(operand, pltpu.HBM if place in loose else pltpu.VMEM)
        for place, operand in enumerate(operands)
    ]
    return pl.pallas_call(
        kernel,
        out_shape=shapes,
        scratch_shapes=scratch,
        in_specs=[
            pl.BlockSpec(memory_space=pltpu.HBM if place in loose else pltpu.VMEM)
            for place in range(len(operands))
        ],
        cost_estimate=pl.CostEstimate(
            flops=micros * 1_000_000_000, bytes_accessed=micros * 3_000_000, transcendentals=0
        ),
        compiler_params=pltpu.CompilerParams(vmem_limit_bytes=VMEM_LIMIT),
        name=name,
    )(*operands)


def on_device(light_field, spatial_weight, epi_weight, upsample_weight, image_grad):
    _, _, views, rows, chans, breadth = light_field.shape
    light = light_field.reshape(views, rows, chans, breadth)
    image = image_grad.reshape(views, image_grad.shape[3], image_grad.shape[4])

    three = 3 * chans
    like = pltpu.VMEM
    plain = jax.ShapeDtypeStruct
    half_out = like((views, 2, chans, breadth), F32)
    taps = like((three, three), BF16)
    edge_line = like((views, 1, chans, breadth), BF16)
    (
        mixed_for_one,
        mixed_for_two,
        dealt,
        inner_out,
        deal,
        spatial_taps,
        epi_taps,
        back_taps,
        drop,
        light_here,
        send_one,
        send_two,
    ) = local_call(
        inner_kernel,
        (
            like((4 * chans + 64, breadth), BF16),
            like((4 * chans + 64, breadth), BF16),
            like((views, 64, breadth), BF16),
            half_out,
            like((512, 512), BF16),
            taps,
            taps,
            like((rows, 4 * chans, 4 * chans), BF16),
            like((rows, chans, 64), BF16),
            like(light.shape, BF16),
            edge_line,
            edge_line,
        ),
        "inner",
        image,
        light,
        spatial_weight,
        epi_weight,
        upsample_weight,
        loose=(0, 1, 2, 3, 4),
        scratch=[
            pltpu.VMEM(image.shape, BF16),
            pltpu.VMEM(spatial_weight.shape, BF16),
            pltpu.VMEM(epi_weight.shape, BF16),
            pltpu.VMEM(upsample_weight.shape, BF16),
            pltpu.SemaphoreType.DMA((5,)),
        ],
    )
    light = light_here
    line_one, line_two = with_next_and_before(send_one, send_two, ROWS)
    mixed_one, mixed_two = with_next_and_before(mixed_for_one, mixed_for_two, "ang")
    first, edge_out = local_call(
        edge_kernel,
        (like((4 * chans, breadth), BF16), half_out),
        "edge",
        light,
        line_one,
        line_two,
        spatial_taps,
    )
    first_one, first_two = with_next_and_before(first, first, "ang")

    lift_half = like((views, 64, breadth), BF16)
    whole_pay = like((640, 128), F32)
    inner_pay, inner_lift, edge_grad = local_call(
        main_inner_kernel,
        (whole_pay, lift_half, like((2, 4, chans, breadth), BF16)),
        "main_inner",
        mixed_for_one,
        mixed_one,
        mixed_two,
        dealt,
        light,
        inner_out,
        epi_taps,
        back_taps,
        drop,
    )
    pay, edge_lift = local_call(
        main_edge_kernel,
        (whole_pay, lift_half),
        "main_edge",
        first,
        first_one,
        first_two,
        dealt,
        edge_grad,
        light,
        line_one,
        line_two,
        edge_out,
        epi_taps,
        back_taps,
        inner_pay,
    )
    up = local_call(
        weave_kernel, plain(image.shape, BF16), "weave", inner_lift, edge_lift, deal
    )
    spatial_grad, epi_grad, up_grad = local_call(
        unpack_kernel,
        (
            plain(spatial_weight.shape, F32),
            plain(epi_weight.shape, F32),
            plain(upsample_weight.shape, F32),
        ),
        "unpack",
        sum_everywhere(pay),
        scratch=[pltpu.VMEM((640, 128), F32)],
    )
    return (up.reshape(image_grad.shape), spatial_grad, epi_grad, up_grad)


def solution(mesh):
    split = Mesh(mesh.devices.reshape(2, 2, 4, 4, 4), ("pair", "core", "ang", "quad", "x"))
    image_spec = P(DP, None, "ang", ROWS, None)
    return jax.shard_map(
        on_device,
        mesh=split,
        in_specs=(P(DP, None, "ang", ROWS, None, None), P(), P(), P(), image_spec),
        out_specs=(image_spec, P(), P(), P()),
        check_vma=False,
    )
```

```python
import jax
import jax.numpy as jnp
from jax import lax
from jax.experimental import pallas as pl
from jax.experimental.pallas import tpu as pltpu
from jax.sharding import Mesh
from jax.sharding import PartitionSpec as P

F32 = jnp.float32
BF16 = jnp.bfloat16
DP = ("pair", "core")
ROWS = ("quad", "x")
VMEM_LIMIT = 40 * 1024 * 1024


def swapped(value, axis, step):
    count = lax.axis_size(axis)
    return lax.ppermute(value, axis, [(i, (i + step) % count) for i in range(count)])


def sum_everywhere(pay):
    plane = ("ang", "x")
    rows = pay.shape[0]
    mine = lax.all_to_all(
        pay.reshape(16, rows // 16, 128), plane, split_axis=0, concat_axis=0, tiled=True
    ).sum(0)
    mine = mine + swapped(mine, "core", 1)
    for flip in (1, 3):
        mine = mine + lax.ppermute(mine, "quad", [(i, i ^ flip) for i in range(4)])
    spread = jnp.broadcast_to(mine.astype(BF16)[None], (32,) + mine.shape)
    gathered = lax.all_to_all(spread, ("pair",) + plane, split_axis=0, concat_axis=0, tiled=True)
    return gathered.reshape(2, rows, 128)


def is_even(axis):
    return lax.axis_index(axis) % 2 == 0


def with_next_and_before(first_send, second_send, axis):
    count = lax.axis_size(axis)
    axes = (axis,) if isinstance(axis, str) else axis
    pairs = [(count - 1, 2 * count - 1), (0, count)]
    for core in (0, count):
        pairs += [(core + i, core + i + 1) for i in range(1, count - 1, 2)]
    two = lax.ppermute(second_send, ("core",) + axes, pairs + [(j, i) for i, j in pairs])
    one = lax.ppermute(first_send, axis, [(i, i ^ 1) for i in range(count)])
    return one, two


def has_neighbours(axis, count):
    place = lax.axis_index(axis)
    return place > 0, place < count - 1


def chosen(flags, one, two):
    even, present = flags
    values = jnp.where(even, one, two)
    return jnp.where(present, values, jnp.zeros_like(values))


def sides(axis, count):
    even = is_even(axis)
    before, after = has_neighbours(axis, count)
    return (jnp.logical_not(even), before), (even, after)


def column(shape):
    return lax.broadcasted_iota(jnp.int32, shape, len(shape) - 1)


def from_left(values):
    rolled = pltpu.roll(values, 1, axis=1)
    return jnp.where(column(values.shape) == 0, jnp.zeros_like(rolled), rolled)


def from_right(values):
    width = values.shape[1]
    rolled = pltpu.roll(values, width - 1, axis=1)
    return jnp.where(column(values.shape) == width - 1, jnp.zeros_like(rolled), rolled)


def product(left, right):
    return jnp.dot(left, right, preferred_element_type=F32)


def product_nt(left, right):
    return lax.dot_general(left, right, (((1,), (1,)), ((), ())), preferred_element_type=F32)


def gate_of(values):
    return 0.5 * jnp.tanh(0.5 * values) + 0.5


def silu_slope(values, gate):
    return gate * (1.0 + values * (1.0 - gate))


def taps_of(slope):
    slope = slope.astype(BF16)
    return jnp.concatenate([from_right(slope), slope, from_left(slope)], axis=0)


def conv_taps(weights, stacked, forward):
    return join_taps(product(weights, stacked), forward)


def join_taps(taps, forward):
    chans = taps.shape[0] // 3
    left, right = (from_left, from_right) if forward else (from_right, from_left)
    return taps[chans : 2 * chans] + left(taps[:chans]) + right(taps[2 * chans :])


def unit(size):
    return jnp.where(
        lax.broadcasted_iota(jnp.int32, (size, size), 0)
        == lax.broadcasted_iota(jnp.int32, (size, size), 1),
        1.0,
        0.0,
    ).astype(BF16)


def forward_taps(ref, taps_ref):
    chans = ref.shape[2]
    for j in range(3):
        taps_ref[j * chans : (j + 1) * chans] = jnp.concatenate([ref[i, j] for i in range(3)], axis=1)


def prepare_weights(spatial_ref, epi_ref, up_ref, taps_ref, epi_taps_ref, back_ref, drop_ref):
    chans = spatial_ref.shape[2]
    forward_taps(spatial_ref, taps_ref)
    forward_taps(epi_ref, epi_taps_ref)
    stacked = jnp.concatenate(
        [jnp.concatenate([epi_ref[2 - s, j] for j in range(3)], axis=1) for s in range(3)], axis=0
    )
    back = product_nt(unit(3 * chans), stacked).astype(BF16)
    turned = product_nt(unit(chans), up_ref[...]).astype(BF16)
    line = lax.broadcasted_iota(jnp.int32, (64, 16), 0)
    sub = lax.broadcasted_iota(jnp.int32, (64, 16), 1)
    match = sub == 4 * (line % 4) + line // 16
    for h in range(4):
        pick = jnp.where(match & ((line % 16) // 4 == h), 1.0, 0.0).astype(BF16)
        lift = product(pick, up_ref[...]).astype(BF16)
        back_ref[h, : 3 * chans] = jnp.concatenate([back, jnp.zeros((3 * chans, 64), BF16)], axis=1)
        back_ref[h, 3 * chans :] = jnp.concatenate(
            [jnp.zeros((64, 3 * chans), BF16), lift], axis=1
        )
        drop_ref[h] = product_nt(turned, pick).astype(BF16)


def inner_kernel(
    image_hbm,
    light_hbm,
    spatial_hbm,
    epi_hbm,
    up_hbm,
    mixed_one_ref,
    mixed_two_ref,
    dealt_ref,
    out_ref,
    deal_ref,
    weight_ref,
    epi_taps_ref,
    back_ref,
    drop_ref,
    light_ref,
    one_ref,
    two_ref,
    image_ref,
    spatial_ref,
    epi_ref,
    up_ref,
    sems,
):
    pairs = (
        (spatial_hbm, spatial_ref),
        (image_hbm, image_ref),
        (light_hbm, light_ref),
        (epi_hbm, epi_ref),
        (up_hbm, up_ref),
    )
    copies = [
        pltpu.make_async_copy(source, target, sems.at[place])
        for place, (source, target) in enumerate(pairs)
    ]
    for copy in copies:
        copy.start()
    size = deal_ref.shape[0]
    source = lax.broadcasted_iota(jnp.int32, (size, size), 0)
    target = lax.broadcasted_iota(jnp.int32, (size, size), 1)
    lanes = size // 4
    wanted = 4 * (target % lanes) + target // lanes
    deal = jnp.where(source == wanted, 1.0, 0.0).astype(BF16)
    deal_ref[...] = deal
    chans = light_ref.shape[2]
    for copy in copies:
        copy.wait()
    even = is_even(ROWS)
    last = light_ref.shape[1] - 1
    for view in range(2):
        one_ref[view, 0] = jnp.where(even, light_ref[view, last], light_ref[view, 0])
        two_ref[view, 0] = jnp.where(even, light_ref[view, 0], light_ref[view, last])
    prepare_weights(
        spatial_ref, epi_ref, up_ref, weight_ref, epi_taps_ref, back_ref, drop_ref
    )
    for block in range(image_ref.shape[2] // size):
        cut = slice(block * size, (block + 1) * size)
        stacked = jnp.concatenate([image_ref[0, :, cut], image_ref[1, :, cut]], axis=0)
        moved = product(stacked, deal).astype(BF16)
        for view in range(2):
            for q in range(4):
                dealt_ref[
                    view, q * 16 : (q + 1) * 16, block * lanes : (block + 1) * lanes
                ] = moved[view * 16 : (view + 1) * 16, q * lanes : (q + 1) * lanes]
    even_view = is_even("ang")
    mixed_one_ref[4 * chans :] = jnp.where(even_view, dealt_ref[1], dealt_ref[0])
    mixed_two_ref[4 * chans :] = jnp.where(even_view, dealt_ref[0], dealt_ref[1])
    for view in range(2):
        for slot, h in enumerate((1, 2)):
            stacked = jnp.concatenate([light_ref[view, h + k] for k in (-1, 0, 1)], axis=0)
            total = conv_taps(weight_ref[...], stacked, True)
            gate = gate_of(total)
            out_ref[view, slot] = silu_slope(total, gate)
            first = (light_ref[view, h].astype(F32) + total * gate).astype(BF16)
            cut = slice((2 * view + slot) * chans, (2 * view + slot + 1) * chans)
            mixed_one_ref[cut] = first
            mixed_two_ref[cut] = first


def edge_kernel(light_ref, two_ref, one_ref, weight_ref, first_ref, out_ref):
    chans = light_ref.shape[2]
    above, below = sides(ROWS, 16)
    for view in range(2):
        for slot, h in enumerate((0, 3)):
            if slot == 0:
                stacked = [chosen(above, one_ref[view, 0], two_ref[view, 0]), light_ref[view, 0], light_ref[view, 1]]
            else:
                stacked = [light_ref[view, 2], light_ref[view, 3], chosen(below, one_ref[view, 0], two_ref[view, 0])]
            total = conv_taps(weight_ref[...], jnp.concatenate(stacked, axis=0), True)
            gate = gate_of(total)
            out_ref[view, slot] = silu_slope(total, gate)
            first = light_ref[view, h].astype(F32) + total * gate
            cut = slice((2 * view + slot) * chans, (2 * view + slot + 1) * chans)
            first_ref[cut] = first.astype(BF16)


def main_rows(rows, firsts, dealt, grad_of, near, out_ref, epi_ref, back_ref, pay_ref, lift_out):
    chans = out_ref.shape[2]
    three = 3 * chans
    lifted = [None, None]
    epi_left, epi_right, spatial_left, spatial_right = [], [], [], []
    before, after = sides("ang", 4)
    for slot, h in enumerate(rows):
        cuts = [slice((2 * v + slot) * chans, (2 * v + slot + 1) * chans) for v in range(2)]
        stack = jnp.concatenate(
            [chosen(before, firsts[1][cut], firsts[2][cut]) for cut in cuts]
            + [firsts[0][cut] for cut in cuts]
            + [chosen(after, firsts[1][cut], firsts[2][cut]) for cut in cuts],
            axis=0,
        )
        here = (lax.broadcasted_iota(jnp.int32, dealt[1].shape, 0) % 16) // 4 == h
        grads, slopes, seconds = [], [], []
        for v in range(4):
            window = stack[v * chans : (v + 3) * chans]
            total = conv_taps(epi_ref[...], window, True)
            gate = gate_of(total)
            grad = grad_of(slot, v).astype(F32)
            slope = grad * silu_slope(total, gate)
            slopes.append(slope.astype(BF16))
            if v in (1, 2):
                grads.append(grad)
                own = stack[(v + 1) * chans : (v + 2) * chans]
                second = (own.astype(F32) + total * gate).astype(BF16)
                seconds.append(second)
                shown = jnp.where(here, dealt[v], jnp.zeros_like(dealt[v]))
                epi_left.append(jnp.concatenate([taps_of(slope), shown], axis=0))
                epi_right.append(jnp.concatenate([window, second], axis=0))
        slopes = jnp.concatenate(slopes, axis=0)
        for v in range(2):
            below = jnp.concatenate([slopes[v * chans : (v + 3) * chans], seconds[v]], axis=0)
            both = product(back_ref[h], below)
            part = both[three:]
            lifted[v] = part if slot == 0 else lifted[v] + part
            first_grad = (grads[v] + join_taps(both[:three], False)).astype(BF16).astype(F32)
            slope = first_grad * out_ref[v, slot]
            spatial_left.append(taps_of(slope))
            spatial_right.append(jnp.concatenate(near(v, h), axis=0))
    for v in range(2):
        lift_out[v] = lifted[v].astype(BF16)
    epi = product_nt(jnp.concatenate(epi_left, axis=1), jnp.concatenate(epi_right, axis=1))
    spatial = product_nt(
        jnp.concatenate(spatial_left, axis=1), jnp.concatenate(spatial_right, axis=1)
    )
    pieces = (
        spatial[:, :128],
        epi[:three, :128],
        jnp.concatenate([spatial[:, 128:], epi[:three, 128:three]], axis=1),
        jnp.concatenate([epi[three:, three:], jnp.zeros((64, 128 - chans), F32)], axis=1),
    )
    start = 0
    for piece in pieces:
        end = start + piece.shape[0]
        pay_ref[start:end] = piece
        start = end


def dealt_views(dealt_ref, one_ref, two_ref, chans):
    before, after = sides("ang", 4)
    one, two = one_ref[4 * chans :], two_ref[4 * chans :]
    return [chosen(before, one, two), dealt_ref[0], dealt_ref[1], chosen(after, one, two)]


def main_inner_kernel(
    own_ref,
    mixed_one_ref,
    mixed_two_ref,
    dealt_ref,
    light_ref,
    out_ref,
    epi_ref,
    back_ref,
    drop_ref,
    pay_ref,
    lift_out,
    edge_grad_ref,
):
    dealt = dealt_views(dealt_ref, mixed_one_ref, mixed_two_ref, light_ref.shape[2])
    for slot, h in enumerate((0, 3)):
        for v in range(4):
            edge_grad_ref[slot, v] = product(drop_ref[h], dealt[v]).astype(BF16)

    def grad_of(slot, v):
        return product(drop_ref[slot + 1], dealt[v]).astype(BF16)

    def near(v, h):
        return [light_ref[v, h + k] for k in (-1, 0, 1)]

    main_rows(
        (1, 2),
        (own_ref, mixed_one_ref, mixed_two_ref),
        dealt,
        grad_of,
        near,
        out_ref,
        epi_ref,
        back_ref,
        pay_ref,
        lift_out,
    )


def main_edge_kernel(
    first_ref,
    first_one_ref,
    first_two_ref,
    dealt_ref,
    edge_grad_ref,
    light_ref,
    two_ref,
    one_ref,
    out_ref,
    epi_ref,
    back_ref,
    inner_pay_ref,
    pay_ref,
    lift_out,
):
    above, below = sides(ROWS, 16)

    def near(v, h):
        if h == 0:
            return [chosen(above, one_ref[v, 0], two_ref[v, 0]), light_ref[v, 0], light_ref[v, 1]]
        return [light_ref[v, 2], light_ref[v, 3], chosen(below, one_ref[v, 0], two_ref[v, 0])]

    main_rows(
        (0, 3),
        (first_ref, first_one_ref, first_two_ref),
        (None, dealt_ref[0], dealt_ref[1], None),
        lambda slot, v: edge_grad_ref[slot, v],
        near,
        out_ref,
        epi_ref,
        back_ref,
        pay_ref,
        lift_out,
    )
    pay_ref[...] += inner_pay_ref[...]


def weave_kernel(inner_ref, edge_ref, deal_ref, up_ref):
    size = deal_ref.shape[0]
    lanes = size // 4
    lifted = [inner_ref[v] + edge_ref[v] for v in range(2)]
    for block in range(up_ref.shape[2] // size):
        spread = [
            jnp.concatenate(
                [
                    lifted[v][q * 16 : (q + 1) * 16, block * lanes : (block + 1) * lanes]
                    for q in range(4)
                ],
                axis=1,
            )
            for v in range(2)
        ]
        woven = product_nt(jnp.concatenate(spread, axis=0), deal_ref[...]).astype(BF16)
        for v in range(2):
            up_ref[v, :, block * size : (block + 1) * size] = woven[v * 16 : (v + 1) * 16]


def unpack_kernel(sent_ref, spatial_ref, epi_ref, up_ref, pay_ref):
    pay_ref[...] = sent_ref[0].astype(F32) + sent_ref[1].astype(F32)
    chans = spatial_ref.shape[2]
    three = 3 * chans
    for which, ref in enumerate((spatial_ref, epi_ref)):
        for j in range(3):
            both = pay_ref[which * three + j * chans : which * three + (j + 1) * chans, :]
            ref[0, j] = both[:, :chans]
            ref[1, j] = both[:, chans:]
            last = pay_ref[2 * three + j * chans : 2 * three + (j + 1) * chans, :]
            ref[2, j] = last[:, which * chans : (which + 1) * chans]
    for p in range(4):
        for q in range(4):
            base = 3 * three + q * 16 + p
            total = pay_ref[base : base + 1, :chans]
            for h in range(1, 4):
                total = total + pay_ref[base + 4 * h : base + 4 * h + 1, :chans]
            up_ref[4 * p + q : 4 * p + q + 1, :] = total


def local_call(kernel, shapes, name, *operands, micros=3, loose=(), scratch=()):
    operands = [
        pltpu.with_memory_space_constraint(operand, pltpu.HBM if place in loose else pltpu.VMEM)
        for place, operand in enumerate(operands)
    ]
    return pl.pallas_call(
        kernel,
        out_shape=shapes,
        scratch_shapes=scratch,
        in_specs=[
            pl.BlockSpec(memory_space=pltpu.HBM if place in loose else pltpu.VMEM)
            for place in range(len(operands))
        ],
        cost_estimate=pl.CostEstimate(
            flops=micros * 1_000_000_000, bytes_accessed=micros * 3_000_000, transcendentals=0
        ),
        compiler_params=pltpu.CompilerParams(vmem_limit_bytes=VMEM_LIMIT),
        name=name,
    )(*operands)


def on_device(light_field, spatial_weight, epi_weight, upsample_weight, image_grad):
    _, _, views, rows, chans, breadth = light_field.shape
    light = light_field.reshape(views, rows, chans, breadth)
    image = image_grad.reshape(views, image_grad.shape[3], image_grad.shape[4])

    three = 3 * chans
    like = pltpu.VMEM
    plain = jax.ShapeDtypeStruct
    half_out = like((views, 2, chans, breadth), F32)
    taps = like((three, three), BF16)
    edge_line = like((views, 1, chans, breadth), BF16)
    (
        mixed_for_one,
        mixed_for_two,
        dealt,
        inner_out,
        deal,
        spatial_taps,
        epi_taps,
        back_taps,
        drop,
        light_here,
        send_one,
        send_two,
    ) = local_call(
        inner_kernel,
        (
            like((4 * chans + 64, breadth), BF16),
            like((4 * chans + 64, breadth), BF16),
            like((views, 64, breadth), BF16),
            half_out,
            like((512, 512), BF16),
            taps,
            taps,
            like((rows, 4 * chans, 4 * chans), BF16),
            like((rows, chans, 64), BF16),
            like(light.shape, BF16),
            edge_line,
            edge_line,
        ),
        "inner",
        image,
        light,
        spatial_weight,
        epi_weight,
        upsample_weight,
        loose=(0, 1, 2, 3, 4),
        scratch=[
            pltpu.VMEM(image.shape, BF16),
            pltpu.VMEM(spatial_weight.shape, BF16),
            pltpu.VMEM(epi_weight.shape, BF16),
            pltpu.VMEM(upsample_weight.shape, BF16),
            pltpu.SemaphoreType.DMA((5,)),
        ],
    )
    light = light_here
    line_one, line_two = with_next_and_before(send_one, send_two, ROWS)
    mixed_one, mixed_two = with_next_and_before(mixed_for_one, mixed_for_two, "ang")
    first, edge_out = local_call(
        edge_kernel,
        (like((4 * chans, breadth), BF16), half_out),
        "edge",
        light,
        line_two,
        line_one,
        spatial_taps,
    )
    first_one, first_two = with_next_and_before(first, first, "ang")

    lift_half = like((views, 64, breadth), BF16)
    whole_pay = like((640, 128), F32)
    inner_pay, inner_lift, edge_grad = local_call(
        main_inner_kernel,
        (whole_pay, lift_half, like((2, 4, chans, breadth), BF16)),
        "main_inner",
        mixed_for_one,
        mixed_one,
        mixed_two,
        dealt,
        light,
        inner_out,
        epi_taps,
        back_taps,
        drop,
    )
    pay, edge_lift = local_call(
        main_edge_kernel,
        (whole_pay, lift_half),
        "main_edge",
        first,
        first_one,
        first_two,
        dealt,
        edge_grad,
        light,
        line_two,
        line_one,
        edge_out,
        epi_taps,
        back_taps,
        inner_pay,
    )
    up = local_call(
        weave_kernel, plain(image.shape, BF16), "weave", inner_lift, edge_lift, deal
    )
    spatial_grad, epi_grad, up_grad = local_call(
        unpack_kernel,
        (
            plain(spatial_weight.shape, F32),
            plain(epi_weight.shape, F32),
            plain(upsample_weight.shape, F32),
        ),
        "unpack",
        sum_everywhere(pay),
        scratch=[pltpu.VMEM((640, 128), F32)],
    )
    return (up.reshape(image_grad.shape), spatial_grad, epi_grad, up_grad)


def solution(mesh):
    split = Mesh(mesh.devices.reshape(2, 2, 4, 4, 4), ("pair", "core", "ang", "quad", "x"))
    image_spec = P(DP, None, "ang", ROWS, None)
    return jax.shard_map(
        on_device,
        mesh=split,
        in_specs=(P(DP, None, "ang", ROWS, None, None), P(), P(), P(), image_spec),
        out_specs=(image_spec, P(), P(), P()),
        check_vma=False,
    )
```

```python
import jax
import jax.numpy as jnp
from jax import lax
from jax.experimental import pallas as pl
from jax.experimental.pallas import tpu as pltpu
from jax.sharding import Mesh
from jax.sharding import PartitionSpec as P

F32 = jnp.float32
BF16 = jnp.bfloat16
DP = ("pair", "core")
ROWS = ("quad", "x")
VMEM_LIMIT = 40 * 1024 * 1024


def swapped(value, axis, step):
    count = lax.axis_size(axis)
    return lax.ppermute(value, axis, [(i, (i + step) % count) for i in range(count)])


def sum_everywhere(pay):
    plane = ("ang", "x")
    rows = pay.shape[0]
    mine = lax.all_to_all(
        pay.reshape(16, rows // 16, 128), plane, split_axis=0, concat_axis=0, tiled=True
    ).sum(0)
    mine = mine + swapped(mine, "core", 1)
    for flip in (1, 3):
        mine = mine + lax.ppermute(mine, "quad", [(i, i ^ flip) for i in range(4)])
    spread = jnp.broadcast_to(mine.astype(BF16)[None], (32,) + mine.shape)
    gathered = lax.all_to_all(spread, ("pair",) + plane, split_axis=0, concat_axis=0, tiled=True)
    return gathered.reshape(2, rows, 128)


def is_even(axis):
    return lax.axis_index(axis) % 2 == 0


def with_next_and_before(first_send, second_send, axis):
    count = lax.axis_size(axis)
    axes = (axis,) if isinstance(axis, str) else axis
    pairs = [(count - 1, 2 * count - 1), (0, count)]
    for core in (0, count):
        pairs += [(core + i, core + i + 1) for i in range(1, count - 1, 2)]
    two = lax.ppermute(second_send, ("core",) + axes, pairs + [(j, i) for i, j in pairs])
    one = lax.ppermute(first_send, axis, [(i, i ^ 1) for i in range(count)])
    return one, two


def has_neighbours(axis, count):
    place = lax.axis_index(axis)
    return place > 0, place < count - 1


def chosen(flags, one, two):
    even, present = flags
    values = jnp.where(even, one, two)
    return jnp.where(present, values, jnp.zeros_like(values))


def sides(axis, count):
    even = is_even(axis)
    before, after = has_neighbours(axis, count)
    return (jnp.logical_not(even), before), (even, after)


def column(shape):
    return lax.broadcasted_iota(jnp.int32, shape, len(shape) - 1)


def from_left(values):
    rolled = pltpu.roll(values, 1, axis=1)
    return jnp.where(column(values.shape) == 0, jnp.zeros_like(rolled), rolled)


def from_right(values):
    width = values.shape[1]
    rolled = pltpu.roll(values, width - 1, axis=1)
    return jnp.where(column(values.shape) == width - 1, jnp.zeros_like(rolled), rolled)


def product(left, right):
    return jnp.dot(left, right, preferred_element_type=F32)


def product_nt(left, right):
    return lax.dot_general(left, right, (((1,), (1,)), ((), ())), preferred_element_type=F32)


def gate_of(values):
    return 0.5 * jnp.tanh(0.5 * values) + 0.5


def silu_slope(values, gate):
    return gate * (1.0 + values * (1.0 - gate))


def taps_of(slope):
    slope = slope.astype(BF16)
    return jnp.concatenate([from_right(slope), slope, from_left(slope)], axis=0)


def conv_taps(weights, stacked, forward):
    return join_taps(product(weights, stacked), forward)


def join_taps(taps, forward):
    chans = taps.shape[0] // 3
    left, right = (from_left, from_right) if forward else (from_right, from_left)
    return taps[chans : 2 * chans] + left(taps[:chans]) + right(taps[2 * chans :])


def unit(size):
    return jnp.where(
        lax.broadcasted_iota(jnp.int32, (size, size), 0)
        == lax.broadcasted_iota(jnp.int32, (size, size), 1),
        1.0,
        0.0,
    ).astype(BF16)


def forward_taps(ref, taps_ref):
    chans = ref.shape[2]
    for j in range(3):
        taps_ref[j * chans : (j + 1) * chans] = jnp.concatenate([ref[i, j] for i in range(3)], axis=1)


def prepare_weights(spatial_ref, epi_ref, up_ref, taps_ref, epi_taps_ref, back_ref, drop_ref):
    chans = spatial_ref.shape[2]
    forward_taps(spatial_ref, taps_ref)
    forward_taps(epi_ref, epi_taps_ref)
    stacked = jnp.concatenate(
        [jnp.concatenate([epi_ref[2 - s, j] for j in range(3)], axis=1) for s in range(3)], axis=0
    )
    back = product_nt(unit(3 * chans), stacked).astype(BF16)
    turned = product_nt(unit(chans), up_ref[...]).astype(BF16)
    line = lax.broadcasted_iota(jnp.int32, (64, 16), 0)
    sub = lax.broadcasted_iota(jnp.int32, (64, 16), 1)
    match = sub == 4 * (line % 4) + line // 16
    for h in range(4):
        pick = jnp.where(match & ((line % 16) // 4 == h), 1.0, 0.0).astype(BF16)
        lift = product(pick, up_ref[...]).astype(BF16)
        back_ref[h, : 3 * chans] = jnp.concatenate([back, jnp.zeros((3 * chans, 64), BF16)], axis=1)
        back_ref[h, 3 * chans :] = jnp.concatenate(
            [jnp.zeros((64, 3 * chans), BF16), lift], axis=1
        )
        drop_ref[h] = product_nt(turned, pick).astype(BF16)


def inner_kernel(
    image_hbm,
    light_hbm,
    spatial_hbm,
    epi_hbm,
    up_hbm,
    mixed_one_ref,
    mixed_two_ref,
    dealt_ref,
    out_ref,
    deal_ref,
    weight_ref,
    epi_taps_ref,
    back_ref,
    drop_ref,
    light_ref,
    one_ref,
    two_ref,
    image_ref,
    spatial_ref,
    epi_ref,
    up_ref,
    sems,
):
    pairs = (
        (spatial_hbm, spatial_ref),
        (image_hbm, image_ref),
        (light_hbm, light_ref),
        (epi_hbm, epi_ref),
        (up_hbm, up_ref),
    )
    copies = [
        pltpu.make_async_copy(source, target, sems.at[place])
        for place, (source, target) in enumerate(pairs)
    ]
    for copy in copies:
        copy.start()
    size = deal_ref.shape[0]
    source = lax.broadcasted_iota(jnp.int32, (size, size), 0)
    target = lax.broadcasted_iota(jnp.int32, (size, size), 1)
    lanes = size // 4
    wanted = 4 * (target % lanes) + target // lanes
    deal = jnp.where(source == wanted, 1.0, 0.0).astype(BF16)
    deal_ref[...] = deal
    chans = light_ref.shape[2]
    for copy in copies:
        copy.wait()
    even = is_even(ROWS)
    last = light_ref.shape[1] - 1
    for view in range(2):
        one_ref[view, 0] = jnp.where(even, light_ref[view, last], light_ref[view, 0])
        two_ref[view, 0] = jnp.where(even, light_ref[view, 0], light_ref[view, last])
    prepare_weights(
        spatial_ref, epi_ref, up_ref, weight_ref, epi_taps_ref, back_ref, drop_ref
    )
    for block in range(image_ref.shape[2] // size):
        cut = slice(block * size, (block + 1) * size)
        stacked = jnp.concatenate([image_ref[0, :, cut], image_ref[1, :, cut]], axis=0)
        moved = product(stacked, deal).astype(BF16)
        for view in range(2):
            for q in range(4):
                dealt_ref[
                    view, q * 16 : (q + 1) * 16, block * lanes : (block + 1) * lanes
                ] = moved[view * 16 : (view + 1) * 16, q * lanes : (q + 1) * lanes]
    even_view = is_even("ang")
    mixed_one_ref[4 * chans :] = jnp.where(even_view, dealt_ref[1], dealt_ref[0])
    mixed_two_ref[4 * chans :] = jnp.where(even_view, dealt_ref[0], dealt_ref[1])
    for view in range(2):
        for slot, h in enumerate((1, 2)):
            stacked = jnp.concatenate([light_ref[view, h + k] for k in (-1, 0, 1)], axis=0)
            total = conv_taps(weight_ref[...], stacked, True)
            gate = gate_of(total)
            out_ref[view, slot] = silu_slope(total, gate)
            first = (light_ref[view, h].astype(F32) + total * gate).astype(BF16)
            cut = slice((2 * view + slot) * chans, (2 * view + slot + 1) * chans)
            mixed_one_ref[cut] = first
            mixed_two_ref[cut] = first


def edge_kernel(light_ref, two_ref, one_ref, weight_ref, first_ref, out_ref):
    chans = light_ref.shape[2]
    above, below = sides(ROWS, 16)
    for view in range(2):
        for slot, h in enumerate((0, 3)):
            if slot == 0:
                stacked = [chosen(above, one_ref[view, 0], two_ref[view, 0]), light_ref[view, 0], light_ref[view, 1]]
            else:
                stacked = [light_ref[view, 2], light_ref[view, 3], chosen(below, one_ref[view, 0], two_ref[view, 0])]
            total = conv_taps(weight_ref[...], jnp.concatenate(stacked, axis=0), True)
            gate = gate_of(total)
            out_ref[view, slot] = silu_slope(total, gate)
            first = light_ref[view, h].astype(F32) + total * gate
            cut = slice((2 * view + slot) * chans, (2 * view + slot + 1) * chans)
            first_ref[cut] = first.astype(BF16)


def main_rows(rows, firsts, dealt, grad_of, near, out_ref, epi_ref, back_ref, pay_ref, lift_out):
    chans = out_ref.shape[2]
    three = 3 * chans
    lifted = [None, None]
    epi_left, epi_right, spatial_left, spatial_right = [], [], [], []
    before, after = sides("ang", 4)
    for slot, h in enumerate(rows):
        cuts = [slice((2 * v + slot) * chans, (2 * v + slot + 1) * chans) for v in range(2)]
        stack = jnp.concatenate(
            [chosen(before, firsts[1][cut], firsts[2][cut]) for cut in cuts]
            + [firsts[0][cut] for cut in cuts]
            + [chosen(after, firsts[1][cut], firsts[2][cut]) for cut in cuts],
            axis=0,
        )
        here = (lax.broadcasted_iota(jnp.int32, dealt[1].shape, 0) % 16) // 4 == h
        grads, slopes, seconds = [], [], []
        for v in range(4):
            window = stack[v * chans : (v + 3) * chans]
            total = conv_taps(epi_ref[...], window, True)
            gate = gate_of(total)
            grad = grad_of(slot, v).astype(F32)
            slope = grad * silu_slope(total, gate)
            slopes.append(slope.astype(BF16))
            if v in (1, 2):
                grads.append(grad)
                own = stack[(v + 1) * chans : (v + 2) * chans]
                second = (own.astype(F32) + total * gate).astype(BF16)
                seconds.append(second)
                shown = jnp.where(here, dealt[v], jnp.zeros_like(dealt[v]))
                epi_left.append(jnp.concatenate([taps_of(slope), shown], axis=0))
                epi_right.append(jnp.concatenate([window, second], axis=0))
        slopes = jnp.concatenate(slopes, axis=0)
        for v in range(2):
            below = jnp.concatenate([slopes[v * chans : (v + 3) * chans], seconds[v]], axis=0)
            both = product(back_ref[h], below)
            part = both[three:]
            lifted[v] = part if slot == 0 else lifted[v] + part
            first_grad = (grads[v] + join_taps(both[:three], False)).astype(BF16).astype(F32)
            slope = first_grad * out_ref[v, slot]
            spatial_left.append(taps_of(slope))
            spatial_right.append(jnp.concatenate(near(v, h), axis=0))
    for v in range(2):
        lift_out[v] = lifted[v].astype(BF16)
    epi = product_nt(jnp.concatenate(epi_left, axis=1), jnp.concatenate(epi_right, axis=1))
    spatial = product_nt(
        jnp.concatenate(spatial_left, axis=1), jnp.concatenate(spatial_right, axis=1)
    )
    pieces = (
        spatial[:, :128],
        epi[:three, :128],
        jnp.concatenate([spatial[:, 128:], epi[:three, 128:three]], axis=1),
        jnp.concatenate([epi[three:, three:], jnp.zeros((64, 128 - chans), F32)], axis=1),
    )
    start = 0
    for piece in pieces:
        end = start + piece.shape[0]
        pay_ref[start:end] = piece
        start = end


def dealt_views(dealt_ref, one_ref, two_ref, chans):
    before, after = sides("ang", 4)
    one, two = one_ref[4 * chans :], two_ref[4 * chans :]
    return [chosen(before, one, two), dealt_ref[0], dealt_ref[1], chosen(after, one, two)]


def main_inner_kernel(
    own_ref,
    mixed_two_ref,
    mixed_one_ref,
    dealt_ref,
    light_ref,
    out_ref,
    epi_ref,
    back_ref,
    drop_ref,
    pay_ref,
    lift_out,
    edge_grad_ref,
):
    dealt = dealt_views(dealt_ref, mixed_one_ref, mixed_two_ref, light_ref.shape[2])
    for slot, h in enumerate((0, 3)):
        for v in range(4):
            edge_grad_ref[slot, v] = product(drop_ref[h], dealt[v]).astype(BF16)

    def grad_of(slot, v):
        return product(drop_ref[slot + 1], dealt[v]).astype(BF16)

    def near(v, h):
        return [light_ref[v, h + k] for k in (-1, 0, 1)]

    main_rows(
        (1, 2),
        (own_ref, mixed_one_ref, mixed_two_ref),
        dealt,
        grad_of,
        near,
        out_ref,
        epi_ref,
        back_ref,
        pay_ref,
        lift_out,
    )


def main_edge_kernel(
    first_ref,
    first_two_ref,
    first_one_ref,
    dealt_ref,
    edge_grad_ref,
    light_ref,
    two_ref,
    one_ref,
    out_ref,
    epi_ref,
    back_ref,
    inner_pay_ref,
    pay_ref,
    lift_out,
):
    above, below = sides(ROWS, 16)

    def near(v, h):
        if h == 0:
            return [chosen(above, one_ref[v, 0], two_ref[v, 0]), light_ref[v, 0], light_ref[v, 1]]
        return [light_ref[v, 2], light_ref[v, 3], chosen(below, one_ref[v, 0], two_ref[v, 0])]

    main_rows(
        (0, 3),
        (first_ref, first_one_ref, first_two_ref),
        (None, dealt_ref[0], dealt_ref[1], None),
        lambda slot, v: edge_grad_ref[slot, v],
        near,
        out_ref,
        epi_ref,
        back_ref,
        pay_ref,
        lift_out,
    )
    pay_ref[...] += inner_pay_ref[...]


def weave_kernel(inner_ref, edge_ref, deal_ref, up_ref):
    size = deal_ref.shape[0]
    lanes = size // 4
    lifted = [inner_ref[v] + edge_ref[v] for v in range(2)]
    for block in range(up_ref.shape[2] // size):
        spread = [
            jnp.concatenate(
                [
                    lifted[v][q * 16 : (q + 1) * 16, block * lanes : (block + 1) * lanes]
                    for q in range(4)
                ],
                axis=1,
            )
            for v in range(2)
        ]
        woven = product_nt(jnp.concatenate(spread, axis=0), deal_ref[...]).astype(BF16)
        for v in range(2):
            up_ref[v, :, block * size : (block + 1) * size] = woven[v * 16 : (v + 1) * 16]


def unpack_kernel(sent_ref, spatial_ref, epi_ref, up_ref, pay_ref):
    pay_ref[...] = sent_ref[0].astype(F32) + sent_ref[1].astype(F32)
    chans = spatial_ref.shape[2]
    three = 3 * chans
    for which, ref in enumerate((spatial_ref, epi_ref)):
        for j in range(3):
            both = pay_ref[which * three + j * chans : which * three + (j + 1) * chans, :]
            ref[0, j] = both[:, :chans]
            ref[1, j] = both[:, chans:]
            last = pay_ref[2 * three + j * chans : 2 * three + (j + 1) * chans, :]
            ref[2, j] = last[:, which * chans : (which + 1) * chans]
    for p in range(4):
        for q in range(4):
            base = 3 * three + q * 16 + p
            total = pay_ref[base : base + 1, :chans]
            for h in range(1, 4):
                total = total + pay_ref[base + 4 * h : base + 4 * h + 1, :chans]
            up_ref[4 * p + q : 4 * p + q + 1, :] = total


def local_call(kernel, shapes, name, *operands, micros=3, loose=(), scratch=()):
    operands = [
        pltpu.with_memory_space_constraint(operand, pltpu.HBM if place in loose else pltpu.VMEM)
        for place, operand in enumerate(operands)
    ]
    return pl.pallas_call(
        kernel,
        out_shape=shapes,
        scratch_shapes=scratch,
        in_specs=[
            pl.BlockSpec(memory_space=pltpu.HBM if place in loose else pltpu.VMEM)
            for place in range(len(operands))
        ],
        cost_estimate=pl.CostEstimate(
            flops=micros * 1_000_000_000, bytes_accessed=micros * 3_000_000, transcendentals=0
        ),
        compiler_params=pltpu.CompilerParams(vmem_limit_bytes=VMEM_LIMIT),
        name=name,
    )(*operands)


def on_device(light_field, spatial_weight, epi_weight, upsample_weight, image_grad):
    _, _, views, rows, chans, breadth = light_field.shape
    light = light_field.reshape(views, rows, chans, breadth)
    image = image_grad.reshape(views, image_grad.shape[3], image_grad.shape[4])

    three = 3 * chans
    like = pltpu.VMEM
    plain = jax.ShapeDtypeStruct
    half_out = like((views, 2, chans, breadth), F32)
    taps = like((three, three), BF16)
    edge_line = like((views, 1, chans, breadth), BF16)
    (
        mixed_for_one,
        mixed_for_two,
        dealt,
        inner_out,
        deal,
        spatial_taps,
        epi_taps,
        back_taps,
        drop,
        light_here,
        send_one,
        send_two,
    ) = local_call(
        inner_kernel,
        (
            like((4 * chans + 64, breadth), BF16),
            like((4 * chans + 64, breadth), BF16),
            like((views, 64, breadth), BF16),
            half_out,
            like((512, 512), BF16),
            taps,
            taps,
            like((rows, 4 * chans, 4 * chans), BF16),
            like((rows, chans, 64), BF16),
            like(light.shape, BF16),
            edge_line,
            edge_line,
        ),
        "inner",
        image,
        light,
        spatial_weight,
        epi_weight,
        upsample_weight,
        loose=(0, 1, 2, 3, 4),
        scratch=[
            pltpu.VMEM(image.shape, BF16),
            pltpu.VMEM(spatial_weight.shape, BF16),
            pltpu.VMEM(epi_weight.shape, BF16),
            pltpu.VMEM(upsample_weight.shape, BF16),
            pltpu.SemaphoreType.DMA((5,)),
        ],
    )
    light = light_here
    line_one, line_two = with_next_and_before(send_one, send_two, ROWS)
    mixed_one, mixed_two = with_next_and_before(mixed_for_one, mixed_for_two, "ang")
    first, edge_out = local_call(
        edge_kernel,
        (like((4 * chans, breadth), BF16), half_out),
        "edge",
        light,
        line_two,
        line_one,
        spatial_taps,
    )
    first_one, first_two = with_next_and_before(first, first, "ang")

    lift_half = like((views, 64, breadth), BF16)
    whole_pay = like((640, 128), F32)
    inner_pay, inner_lift, edge_grad = local_call(
        main_inner_kernel,
        (whole_pay, lift_half, like((2, 4, chans, breadth), BF16)),
        "main_inner",
        mixed_for_one,
        mixed_two,
        mixed_one,
        dealt,
        light,
        inner_out,
        epi_taps,
        back_taps,
        drop,
    )
    pay, edge_lift = local_call(
        main_edge_kernel,
        (whole_pay, lift_half),
        "main_edge",
        first,
        first_two,
        first_one,
        dealt,
        edge_grad,
        light,
        line_two,
        line_one,
        edge_out,
        epi_taps,
        back_taps,
        inner_pay,
    )
    up = local_call(
        weave_kernel, plain(image.shape, BF16), "weave", inner_lift, edge_lift, deal
    )
    spatial_grad, epi_grad, up_grad = local_call(
        unpack_kernel,
        (
            plain(spatial_weight.shape, F32),
            plain(epi_weight.shape, F32),
            plain(upsample_weight.shape, F32),
        ),
        "unpack",
        sum_everywhere(pay),
        scratch=[pltpu.VMEM((640, 128), F32)],
    )
    return (up.reshape(image_grad.shape), spatial_grad, epi_grad, up_grad)


def solution(mesh):
    split = Mesh(mesh.devices.reshape(2, 2, 4, 4, 4), ("pair", "core", "ang", "quad", "x"))
    image_spec = P(DP, None, "ang", ROWS, None)
    return jax.shard_map(
        on_device,
        mesh=split,
        in_specs=(P(DP, None, "ang", ROWS, None, None), P(), P(), P(), image_spec),
        out_specs=(image_spec, P(), P(), P()),
        check_vma=False,
    )
```
